32 devices in a mesh: gx: 2 (over x), gy: 4 (over y, core), gz: 4 (over z).
Axes of the slice: x: 2, y: 2, z: 4, core: 2. Of those that a mesh axis runs over, the one named last changes fastest.
Arguments:
- positions: float32 [2, 4, 8, 3, 128], P('gx', 'gy', 'gz'), may hold values from 0 to 8, as said below
- block_fill: int32 [2, 4, 8], P('gx', 'gy', 'gz'), may hold values from 16 to 128, as said below
- noise: float32 [2, 4, 8, 8, 384], P('gx', 'gy', 'gz'), may hold values from -6 to 6
- pair_list: int32 [2, 4, 4, 3, 54], P('gx', 'gy', 'gz'), may hold values from 0 to 26, as said below
- pair_count: int32 [2, 4, 4], P('gx', 'gy', 'gz'), may hold values from 2 to 36, as said below
Outputs:
- displacement: float32 [2, 4, 8, 8, 384], P('gx', 'gy', 'gz')
The draws below stay inside these ranges and needn't reach their ends.
Inputs may be any that keep to these rules, and one draw needn't show every extreme that they name: `positions`: each bead of cell (x, y, z) lies in the unit cube with corner (x, y, z). `block_fill`: beads of a block occupy its first slots. `pair_list`: in each device's list, the first pair_count slots hold field 0, a block index below 2; field 1, a neighbour code 9 (dx + 1) + 3 (dy + 1) + (dz + 1) with dx, dy, dz in -1..1 whose cell lies inside the grid; field 2, the owner flag. The relation is symmetric: a pair is listed on the first block's device exactly when the reverse pair is listed on the second block's device, and exactly one of the two carries owner flag 1; every block lists itself with code 13 and flag 1. Later slots hold 0, 13, 0. `pair_count`: counts the listed pairs of the device, each block's own pair included; some device lists every neighbour inside the grid of each of its blocks.
All inputs are finite; a program needn't handle non-finite values.
Results may differ from the reference program's by a relative error of at most 0.0025.
Values may be sent and summed in bfloat16 or wider, within the bound.
No kernel may reach another device: no remote copies, remote signals or barrier semaphores. Data moves between devices by JAX's collectives and lax.ppermute only.
A program may use at most 64 MiB of HBM per device.

```python
import jax
import jax.numpy as jnp
from jax import lax

BEAD = 128
BLK_Z = 2
SAMPLES = 8
ITERS = 3
ROOT_ITERS = 12
NX = 2
NY = 4
NZ = 8
PAIR_CAP = 54
N_GX = 2
N_GY = 4
N_GZ = 4


def draw_positions(key, part):
    jitter = jax.random.uniform(key, (NX, NY, NZ, 3, BEAD), jnp.float32)
    corner = jnp.stack([lax.broadcasted_iota(jnp.float32, (NX, NY, NZ), axis_number) for axis_number in range(3)], axis=3)
    return corner[..., None] + jitter


def draw_block_fill(key, part):
    first_index = lax.broadcasted_iota(jnp.int32, (NX, NY, NZ), 0)
    lower_bound = BEAD // 8 + 5 * BEAD // 8 * first_index // max(NX - 1, 1)
    spread_draw = jax.random.randint(key, (NX, NY, NZ), 0, BEAD // 4 + 1)
    return (lower_bound + spread_draw).astype(jnp.int32)


def pair_tables(key):
    level_key, test_key, owner_key = jax.random.split(key, 3)
    devices_z = NZ // BLK_Z
    level_draw = jax.random.randint(level_key, (NX, NY, devices_z), 0, 101)
    device_level = level_draw * level_draw // 100
    device_level = device_level.at[NX // 2, NY // 2, devices_z // 2].set(100)
    cell_level = jnp.repeat(device_level, BLK_Z, axis=2)
    pair_tests = jax.random.randint(test_key, (27, NX, NY, NZ), 0, 100)
    coin_flips = jax.random.randint(owner_key, (27, NX, NY, NZ), 0, 2)
    coord_x = lax.broadcasted_iota(jnp.int32, (NX, NY, NZ), 0)
    coord_y = lax.broadcasted_iota(jnp.int32, (NX, NY, NZ), 1)
    coord_z = lax.broadcasted_iota(jnp.int32, (NX, NY, NZ), 2)
    live_list = []
    owner_list = []
    for neighbour_code in range(27):
        shift_x = neighbour_code // 9 - 1
        shift_y = neighbour_code // 3 % 3 - 1
        shift_z = neighbour_code % 3 - 1
        inside = (coord_x + shift_x >= 0) & (coord_x + shift_x < NX) & (coord_y + shift_y >= 0) & (coord_y + shift_y < NY) & (coord_z + shift_z >= 0) & (coord_z + shift_z < NZ)
        partner_level = jnp.roll(cell_level, (-shift_x, -shift_y, -shift_z), axis=(0, 1, 2))
        pair_level = jnp.maximum(cell_level, partner_level)
        if neighbour_code == 13:
            live_now = jnp.ones((NX, NY, NZ), jnp.int32)
            owner_now = jnp.ones((NX, NY, NZ), jnp.int32)
        elif neighbour_code > 13:
            live_now = (inside & (pair_tests[neighbour_code] < pair_level)).astype(jnp.int32)
            owner_now = coin_flips[neighbour_code]
        else:
            mirror_code = 26 - neighbour_code
            mirror_test = jnp.roll(pair_tests[mirror_code], (-shift_x, -shift_y, -shift_z), axis=(0, 1, 2))
            live_now = (inside & (mirror_test < pair_level)).astype(jnp.int32)
            owner_now = 1 - jnp.roll(coin_flips[mirror_code], (-shift_x, -shift_y, -shift_z), axis=(0, 1, 2))
        live_list.append(live_now)
        owner_list.append(owner_now)
    flat_live = jnp.stack(live_list, axis=3).reshape(NX, NY, devices_z, PAIR_CAP)
    flat_owner = jnp.stack(owner_list, axis=3).reshape(NX, NY, devices_z, PAIR_CAP)
    slot_ids = lax.broadcasted_iota(jnp.int32, flat_live.shape, 3)
    ranking = jnp.where(flat_live == 1, slot_ids, slot_ids + PAIR_CAP)
    ranked_order = jnp.argsort(ranking, axis=3, stable=True).astype(jnp.int32)
    sorted_live = jnp.take_along_axis(flat_live, ranked_order, axis=3)
    block_index = jnp.where(sorted_live == 1, ranked_order // 27, 0)
    code_field = jnp.where(sorted_live == 1, ranked_order % 27, 13)
    owner_field = jnp.where(sorted_live == 1, jnp.take_along_axis(flat_owner, ranked_order, axis=3), 0)
    table = jnp.stack([block_index, code_field, owner_field], axis=3).astype(jnp.int32)
    totals = jnp.sum(flat_live, axis=3).astype(jnp.int32)
    return (table, totals)


def draw_pair_list(key, part):
    table, totals = pair_tables(jax.random.fold_in(key, 11))
    return table


def draw_pair_count(key, part):
    table, totals = pair_tables(jax.random.fold_in(key, 11))
    return totals


def levels(key, extent, shards, low, top_value):
    level, own = 1.0, jax.random.fold_in(key, 6)
    for position, parts in shards:
        steps = jnp.exp(jax.random.uniform(jax.random.fold_in(own, position), (parts,), jnp.float32, low / len(shards), top_value / len(shards)))
        level = level * jnp.repeat(steps, extent[position] // parts).reshape([-1 if axis == position else 1 for axis in range(len(extent))])
    return level


def normal_values(stream_key, shape, spread, reach, shards=(), held_as=jnp.bfloat16):
    drawn = spread * jax.random.normal(stream_key, shape, jnp.float32)
    if shards:
        drawn = drawn * levels(stream_key, shape, shards, -0.22, 0.18)
    return jnp.clip(drawn, -reach, reach).astype(held_as)


def setup_inputs(seed: int = 0) -> dict:
    key_of = jax.random.split(jax.random.key(seed), 6)
    positions = draw_positions(jax.random.fold_in(key_of[5], 71), 0)
    block_fill = draw_block_fill(jax.random.fold_in(key_of[5], 71), 0)
    noise = normal_values(key_of[2], (NX, NY, NZ, SAMPLES, 3 * BEAD), 1.0, 6.0, ((0, 2), (1, 4), (2, 4)), jnp.float32)
    pair_list = draw_pair_list(jax.random.fold_in(key_of[5], 71), 0)
    pair_count = draw_pair_count(jax.random.fold_in(key_of[5], 71), 0)
    return {"positions": positions, "block_fill": block_fill, "noise": noise, "pair_list": pair_list, "pair_count": pair_count}


radius = 0.08
floor_sq = 0.0001
epsilon = 1e-06
group_pairs = 32

def mobility_tiles(first_pos, second_pos):
    offset = second_pos[:, :, None, :] - first_pos[:, :, :, None]
    dist_sq = offset[:, 0] * offset[:, 0] + offset[:, 1] * offset[:, 1] + offset[:, 2] * offset[:, 2]
    inverse_sq = 1.0 / jnp.maximum(dist_sq, floor_sq)
    distance = jnp.sqrt(dist_sq)
    reach_ratio = radius * jnp.sqrt(inverse_sq)
    far_iso = 0.75 * reach_ratio * (1.0 + 2.0 / 3.0 * radius * radius * inverse_sq)
    far_dyad = 0.75 * reach_ratio * (1.0 - 2.0 * radius * radius * inverse_sq)
    near_iso = 1.0 - 9.0 / 32.0 * distance / radius
    near_dyad = 3.0 / 32.0 * distance / radius
    apart = dist_sq >= 4.0 * radius * radius
    isotropic = jnp.where(apart, far_iso, near_iso)
    dyadic = jnp.where(apart, far_dyad, near_dyad) * inverse_sq
    identity_three = jnp.eye(3, dtype=jnp.float32)
    offset_t = jnp.transpose(offset, (0, 2, 1, 3))
    product = offset[:, :, :, None, :] * offset_t[:, None, :, :, :]
    mobility = identity_three[None, :, None, :, None] * isotropic[:, None, :, None, :] + dyadic[:, None, :, None, :] * product
    group_size = first_pos.shape[0]
    bead_count = first_pos.shape[2]
    return mobility.reshape(group_size, 3 * bead_count, 3 * bead_count).astype(jnp.bfloat16)

def inverse_three(matrix):
    cofactor = [[matrix[(line_index + 1) % 3][(place_index + 1) % 3] * matrix[(line_index + 2) % 3][(place_index + 2) % 3] - matrix[(line_index + 1) % 3][(place_index + 2) % 3] * matrix[(line_index + 2) % 3][(place_index + 1) % 3] for place_index in range(3)] for line_index in range(3)]
    determinant = matrix[0][0] * cofactor[0][0] + matrix[0][1] * cofactor[0][1] + matrix[0][2] * cofactor[0][2]
    return [[cofactor[place_index][line_index] / determinant for place_index in range(3)] for line_index in range(3)]

def root_first_column(diagonal, coupling):
    zero_entry = jnp.zeros_like(diagonal[0])
    one_entry = jnp.ones_like(diagonal[0])
    trace_scale = (diagonal[0] + diagonal[1] + diagonal[2]) / 3.0
    tridiagonal = [[diagonal[0], coupling[0], zero_entry], [coupling[0], diagonal[1], coupling[1]], [zero_entry, coupling[1], diagonal[2]]]
    root_guess = [[matrix_entry / trace_scale for matrix_entry in matrix_line] for matrix_line in tridiagonal]
    partner = [[one_entry if line_index == place_index else zero_entry for place_index in range(3)] for line_index in range(3)]
    for repeat_index in range(ROOT_ITERS):
        inverse_partner = inverse_three(partner)
        inverse_guess = inverse_three(root_guess)
        root_guess, partner = ([[0.5 * (root_guess[line_index][place_index] + inverse_partner[line_index][place_index]) for place_index in range(3)] for line_index in range(3)], [[0.5 * (partner[line_index][place_index] + inverse_guess[line_index][place_index]) for place_index in range(3)] for line_index in range(3)])
    root_scale = jnp.sqrt(trace_scale)
    return [root_scale * root_guess[line_index][0] for line_index in range(3)]

def local_dot(left, right):
    return lax.optimization_barrier(jnp.sum(left * right, axis=(0, 1, 2, 4)))

def reference(positions, block_fill, noise, pair_list, pair_count):
    row_width = 3 * BEAD
    cell_total = NX * NY * NZ
    bead_slots = lax.broadcasted_iota(jnp.int32, (NX, NY, NZ, BEAD), 3)
    live_mask = jnp.tile((bead_slots < block_fill[..., None]).astype(jnp.float32), (1, 1, 1, 3))[:, :, :, None, :]
    flat_pos = positions.reshape(cell_total, 3, BEAD)
    padded_pos = jnp.pad(positions, ((1, 1), (1, 1), (1, 1), (0, 0), (0, 0))).reshape(-1, 3, BEAD)
    block_ids = pair_list[:, :, :, 0, :]
    neighbour_codes = pair_list[:, :, :, 1, :]
    list_shape = block_ids.shape
    device_x = lax.broadcasted_iota(jnp.int32, list_shape, 0)
    device_y = lax.broadcasted_iota(jnp.int32, list_shape, 1)
    device_z = lax.broadcasted_iota(jnp.int32, list_shape, 2)
    slot_ids = lax.broadcasted_iota(jnp.int32, list_shape, 3)
    valid_mask = (slot_ids < pair_count[..., None]).astype(jnp.float32)
    cell_z = device_z * BLK_Z + block_ids
    home_cells = (device_x * NY + device_y) * NZ + cell_z
    away_cells = ((device_x + neighbour_codes // 9) * (NY + 2) + device_y + neighbour_codes // 3 % 3) * (NZ + 2) + cell_z + neighbour_codes % 3
    entry_total = N_GX * N_GY * N_GZ * PAIR_CAP
    group_count = (entry_total + group_pairs - 1) // group_pairs
    padding_size = group_count * group_pairs - entry_total

    def arrange(values):
        return jnp.pad(values.reshape(-1), (0, padding_size)).reshape(group_count, group_pairs)
    home_groups = arrange(home_cells.astype(jnp.int32))
    away_groups = arrange(away_cells.astype(jnp.int32))
    weight_groups = arrange(valid_mask)

    def apply_mobility(vector_bf):
        padded = jnp.pad(vector_bf, ((1, 1), (1, 1), (1, 1), (0, 0), (0, 0))).reshape(-1, SAMPLES, row_width)

        def accumulate(running, group_data):
            home_pick, away_pick, weight_pick = group_data
            mobility = mobility_tiles(flat_pos[home_pick], padded_pos[away_pick])
            contribution = jnp.einsum('gsk,gmk->gsm', padded[away_pick].astype(jnp.float32), mobility.astype(jnp.float32), precision=lax.Precision.HIGHEST)
            return (running.at[home_pick].add(contribution * weight_pick[:, None, None]), None)
        running, unused = lax.scan(accumulate, jnp.zeros((cell_total, SAMPLES, row_width), jnp.float32), (home_groups, away_groups, weight_groups))
        return running.reshape(NX, NY, NZ, SAMPLES, row_width) * live_mask
    start_vec = noise * live_mask
    start_norm = jnp.sqrt(local_dot(start_vec, start_vec) + epsilon)
    current = start_vec / start_norm[:, None]
    previous = jnp.zeros_like(current)
    beta_prev = jnp.zeros((SAMPLES,), jnp.float32)
    basis = []
    diagonal = []
    coupling = []
    for repeat_index in range(ITERS):
        basis.append(current)
        image_vec = apply_mobility(current.astype(jnp.bfloat16))
        alpha_now = local_dot(current, image_vec)
        diagonal.append(alpha_now)
        if repeat_index + 1 < ITERS:
            residual = image_vec - alpha_now[:, None] * current - beta_prev[:, None] * previous
            beta_now = jnp.sqrt(local_dot(residual, residual) + epsilon)
            coupling.append(beta_now)
            previous = current
            current = residual / beta_now[:, None]
            beta_prev = beta_now
    weights = root_first_column(diagonal, coupling)
    result = (start_norm * weights[0])[:, None] * basis[0]
    for repeat_index in range(1, ITERS):
        result = result + (start_norm * weights[repeat_index])[:, None] * basis[repeat_index]
    return result
```

```python
import functools

import jax
import jax.numpy as jnp
from jax import lax
from jax.experimental import pallas as pl
from jax.experimental.pallas import tpu as pltpu
from jax.sharding import PartitionSpec as P

ITERS = 3
ROOT_ITERS = 12
GROUP = 4
CHUNK = 32

radius = 0.08
floor_sq = 0.0001
epsilon = 1e-06

AXES = ("gx", "gy", "gz")
VMEM = pl.BlockSpec(memory_space=pltpu.VMEM)
SMEM = pl.BlockSpec(memory_space=pltpu.SMEM)
f32 = jnp.float32
bf16 = jnp.bfloat16


def matching(count, parity):
    pairs = []
    for i in range(parity, count - 1, 2):
        pairs += [(i, i + 1), (i + 1, i)]
    return pairs


def swaps(axis, first, second):
    count = lax.axis_size(axis)
    got = [lax.ppermute(first, axis, matching(count, 0))]
    if count > 2:
        got.append(lax.ppermute(second, axis, matching(count, 1)))
    return got


def spread(field):
    blocks, rows, width = field.shape
    columns = jnp.stack([field] + swaps("gx", field, field))
    odd = lax.axis_index("gz") % 2 == 1
    low, high = columns[:, 0], columns[:, blocks - 1]
    got = swaps("gz", jnp.where(odd, low, high), jnp.where(odd, high, low))
    while len(got) < 2:
        got.append(jnp.zeros_like(got[0]))
    deep = jnp.concatenate([columns] + [g[:, None] for g in got], axis=1)
    deep = deep.reshape(-1, rows, width)
    return [deep] + swaps("gy", deep, deep)


def partner(axis, step):
    if lax.axis_size(axis) == 2:
        return jnp.where(step == 0, 0, 1)
    odd = lax.axis_index(axis) % 2
    return jnp.where(step == 0, 0, jnp.where((step < 0) == (odd == 1), 1, 2))


def pair_table(pair_list, pair_count, blocks, columns, zero_slot):
    home, code = pair_list[0, 0, 0, 0], pair_list[0, 0, 0, 1]
    capacity = home.shape[0]
    step_x, step_y, step_z = code // 9 - 1, code // 3 % 3 - 1, code % 3 - 1
    z = home + step_z
    odd = lax.axis_index("gz") % 2
    below = jnp.where(odd == 1, blocks, blocks + 1)
    above = jnp.where(odd == 1, blocks + 1, blocks)
    if lax.axis_size("gz") == 2:
        below = above = blocks
    z = jnp.where(z < 0, below, jnp.where(z >= blocks, above, z))
    slot = (partner("gy", step_y) * columns + partner("gx", step_x)) * (blocks + 2) + z
    live = lax.iota(jnp.int32, capacity) < pair_count[0, 0, 0]
    pad = -capacity % GROUP
    home = jnp.pad(jnp.where(live, home, 0), (0, pad))
    slot = jnp.pad(jnp.where(live, slot, zero_slot), (0, pad), constant_values=zero_slot)
    return jnp.stack([home, slot])


def lane_mask(fill_ref, block, width, beads):
    lanes = lax.broadcasted_iota(jnp.int32, (1, width), 1)
    return (lax.rem(lanes, beads) < fill_ref[block]).astype(f32)


def pack_kernel(fill_ref, noise_ref, pos_ref, start_ref, pack_ref):
    blocks, samples, width = noise_ref.shape
    beads = pos_ref.shape[2]
    for block in range(blocks):
        start = noise_ref[block] * lane_mask(fill_ref, block, width, beads)
        start_ref[block] = start
        pos = jnp.concatenate([pos_ref[block, c : c + 1, :] for c in range(3)], axis=1)
        high = pos.astype(bf16).astype(f32)
        rest = pos - high
        mid = rest.astype(bf16).astype(f32)
        low = rest - mid
        row = lax.broadcasted_iota(jnp.int32, (8, width), 0)
        place = jnp.where(row == 0, high, jnp.where(row == 1, mid, jnp.where(row == 2, low, 0.0)))
        pack_ref[block] = jnp.concatenate([start, place], axis=0).astype(bf16)


def gather_slots(parts, slots_ref):
    count = parts[0].shape[0]
    for i, part in enumerate(parts):
        slots_ref[pl.ds(i * count, count)] = part[...]
    slots_ref[len(parts) * count] = jnp.zeros(slots_ref.shape[1:], bf16)


def position_of(slots_ref, slot, samples, beads):
    rows = slots_ref[slot].astype(f32)[samples : samples + 8]
    pos = rows[0:1] + rows[1:2] + rows[2:3]
    return [pos[:, c * beads : (c + 1) * beads] for c in range(3)]


def make_tile(table_ref, slots_ref, tiles_ref, home_slot, pair, samples, beads):
    home = position_of(slots_ref, home_slot + table_ref[0, pair], samples, beads)
    away = position_of(slots_ref, table_ref[1, pair], samples, beads)
    row = lax.broadcasted_iota(jnp.int32, (8, beads), 0)
    stacked = jnp.where(row == 0, away[0], jnp.where(row == 1, away[1], away[2]))
    turned = jnp.transpose(stacked)
    for first in range(0, beads, CHUNK):
        d = [turned[first : first + CHUNK, c : c + 1] - home[c] for c in range(3)]
        dist_sq = d[0] * d[0] + d[1] * d[1] + d[2] * d[2]
        root = lax.rsqrt(jnp.maximum(dist_sq, 1e-30))
        distance = dist_sq * root
        inv_root = jnp.minimum(root, floor_sq**-0.5)
        inverse_sq = inv_root * inv_root
        far = (0.75 * radius) * inv_root
        far_two = (2.0 * radius * radius) * (far * inverse_sq)
        apart = dist_sq >= 4.0 * radius * radius
        isotropic = jnp.where(apart, far + far_two * (1.0 / 3.0), 1.0 - (9.0 / 32.0 / radius) * distance)
        dyadic = jnp.where(apart, far - far_two, (3.0 / 32.0 / radius) * distance) * inverse_sq
        scaled = [dyadic * d[c] for c in range(3)]
        for c in range(3):
            for e in range(c, 3):
                entry = scaled[c] * d[e]
                if c == e:
                    entry = entry + isotropic
                entry = entry.astype(bf16)
                tiles_ref[pair, pl.ds(e * beads + first, CHUNK), pl.ds(c * beads, beads)] = entry
                if c != e:
                    tiles_ref[pair, pl.ds(c * beads + first, CHUNK), pl.ds(e * beads, beads)] = entry


def multiply(total, table_ref, slots_ref, tiles_ref, sum_ref, samples):
    sum_ref[...] = jnp.zeros_like(sum_ref)

    def group(turn, carry):
        products = []
        for i in range(GROUP):
            pair = turn * GROUP + i
            field = slots_ref[table_ref[1, pair]][:samples]
            tile = tiles_ref[jnp.minimum(pair, total - 1)]
            products.append(jnp.dot(field, tile, preferred_element_type=f32))
        for i in range(GROUP):
            home = table_ref[0, turn * GROUP + i]
            sum_ref[home] = sum_ref[home] + products[i]
        return carry

    lax.fori_loop(0, (total + GROUP - 1) // GROUP, group, 0)


def first_kernel(parts, home_slot, beads, count_ref, fill_ref, table_ref, start_ref, *refs):
    given, (tiles_ref, next_ref, send_ref, slots_ref, sum_ref) = refs[:parts], refs[parts:]
    blocks, samples, width = start_ref.shape
    total = count_ref[0]
    gather_slots(given, slots_ref)

    def make(pair, carry):
        make_tile(table_ref, slots_ref, tiles_ref, home_slot, pair, samples, beads)
        return carry

    lax.fori_loop(0, total, make, 0)
    multiply(total, table_ref, slots_ref, tiles_ref, sum_ref, samples)
    for block in range(blocks):
        new = sum_ref[block] * lane_mask(fill_ref, block, width, beads) - start_ref[block]
        next_ref[block] = new
        send_ref[block] = new.astype(bf16)


def next_kernel(parts, beads, count_ref, fill_ref, table_ref, tiles_ref, old_ref, *refs):
    given, (next_ref, send_ref, slots_ref, sum_ref) = refs[:parts], refs[parts:]
    blocks, samples, width = old_ref.shape
    gather_slots(given, slots_ref)
    multiply(count_ref[0], table_ref, slots_ref, tiles_ref, sum_ref, samples)
    for block in range(blocks):
        new = sum_ref[block] * lane_mask(fill_ref, block, width, beads) - old_ref[block]
        next_ref[block] = new
        send_ref[block] = new.astype(bf16)


MOMENTS = ((0, 0), (0, 1), (1, 1), (1, 2), (2, 2), (2, 3))


def last_kernel(parts, beads, count_ref, fill_ref, table_ref, tiles_ref, x0_ref, x1_ref, x2_ref, *refs):
    given, (moment_ref, slots_ref, sum_ref) = refs[:parts], refs[parts:]
    blocks, samples, width = x0_ref.shape
    gather_slots(given, slots_ref)
    multiply(count_ref[0], table_ref, slots_ref, tiles_ref, sum_ref, samples)
    lanes = moment_ref.shape[2]
    lane = lax.broadcasted_iota(jnp.int32, (samples, lanes), 1)
    row = lax.broadcasted_iota(jnp.int32, (samples, lanes), 0)
    sums = [0.0] * len(MOMENTS)
    for block in range(blocks):
        x = [x0_ref[block], x1_ref[block], x2_ref[block]]
        x.append(sum_ref[block] * lane_mask(fill_ref, block, width, beads) - x[2])
        for k, (i, j) in enumerate(MOMENTS):
            sums[k] = sums[k] + x[i] * x[j]
    grid = jnp.zeros((samples, lanes), f32)
    for k, value in enumerate(sums):
        value = jnp.sum(value, axis=1, keepdims=True)
        grid = jnp.where(lane == row + k * samples, value, grid)
    line = jnp.sum(grid, axis=0, keepdims=True)
    moment_ref[...] = jnp.broadcast_to(line[None], moment_ref.shape)


def inverse_symmetric(m):
    a, b, c, d, e, f = m
    ca, cb, cc = d * f - e * e, c * e - b * f, b * e - c * d
    scale = 1.0 / (a * ca + b * cb + c * cc)
    return (ca * scale, cb * scale, cc * scale, (a * f - c * c) * scale, (b * c - a * e) * scale, (a * d - b * b) * scale)


def final_kernel(moment_ref, x0_ref, x1_ref, x2_ref, out_ref):
    blocks, samples, width = x0_ref.shape
    lanes = moment_ref.shape[2]
    lane = lax.broadcasted_iota(jnp.int32, (samples, lanes), 1)
    row = lax.broadcasted_iota(jnp.int32, (samples, lanes), 0)
    line = jnp.broadcast_to(jnp.sum(moment_ref[...], axis=0), (samples, lanes))
    m00, m01, m11, m12, m22, m23 = [
        jnp.broadcast_to(
            jnp.sum(jnp.where(lane == row + k * samples, line, 0.0), axis=1, keepdims=True), (samples, lanes)
        )
        for k in range(len(MOMENTS))
    ]
    norm_sq = m00 + epsilon
    start_norm = jnp.sqrt(norm_sq)
    inv_sq = 1.0 / norm_sq
    alpha1 = (m00 + m01) * inv_sq
    c = 1.0 - alpha1
    res_sq = (m11 + c * (2.0 * m01 + c * m00)) * inv_sq
    beta1 = jnp.sqrt(jnp.maximum(res_sq, 0.0) + epsilon)
    k2 = 1.0 / (start_norm * beta1)
    n11 = m11 + c * (2.0 * m01 + c * m00)
    n12 = m12 + c * (2.0 * m11 + c * m01)
    alpha2 = k2 * k2 * (n11 + n12)
    f1 = 1.0 + c - alpha2
    f0 = c - alpha2 * c - beta1 * beta1
    n22 = m22 + f1 * (2.0 * m12 + f1 * m11) + f0 * (2.0 * (m11 + f1 * m01) + f0 * m00)
    beta2 = jnp.sqrt(jnp.maximum(k2 * k2 * n22, 0.0) + epsilon)
    k3 = k2 / beta2
    n23 = m23 + f1 * (2.0 * m22 + f1 * m12) + f0 * (2.0 * (m12 + f1 * m11) + f0 * m01)
    alpha3 = k3 * k3 * (jnp.maximum(n22, 0.0) + n23)

    scale = (alpha1 + alpha2 + alpha3) / 3.0
    inv_scale = 1.0 / scale
    zero, one = jnp.zeros_like(scale), jnp.ones_like(scale)
    y = (alpha1 * inv_scale, beta1 * inv_scale, zero, alpha2 * inv_scale, beta2 * inv_scale, alpha3 * inv_scale)
    z = (one, zero, zero, one, zero, one)
    for _ in range(ROOT_ITERS):
        inv_z, inv_y = inverse_symmetric(z), inverse_symmetric(y)
        y = tuple(0.5 * (p + q) for p, q in zip(y, inv_z))
        z = tuple(0.5 * (p + q) for p, q in zip(z, inv_y))
    root_scale = jnp.sqrt(scale)
    r1, r2, r3 = root_scale * y[0], root_scale * y[1], root_scale * y[2]
    w2, w3 = start_norm * r2 * k2, start_norm * r3 * k3
    p0 = r1 + w2 * c + w3 * f0
    p1 = w2 + w3 * f1
    for block in range(blocks):
        for first in range(0, width, lanes):
            at = pl.ds(first, lanes)
            out_ref[block, :, at] = p0 * x0_ref[block, :, at] + p1 * x1_ref[block, :, at] + w3 * x2_ref[block, :, at]


def call(kernel, outs, in_specs, scratch=(), limit=None, cost=None):
    return pl.pallas_call(
        kernel,
        out_shape=outs,
        in_specs=in_specs,
        out_specs=jax.tree.map(lambda _: VMEM, outs),
        scratch_shapes=list(scratch),
        compiler_params=pltpu.CompilerParams(vmem_limit_bytes=limit),
        cost_estimate=cost,
    )


def body(positions, block_fill, noise, pair_list, pair_count):
    blocks, beads = positions.shape[2], positions.shape[4]
    samples, width = noise.shape[3], noise.shape[4]
    shape = (blocks, samples, width)
    devices = lax.axis_size(AXES)
    columns = 2 if lax.axis_size("gx") == 2 else 3
    rows_y = 2 if lax.axis_size("gy") == 2 else 3
    per_part = columns * (blocks + 2)
    zero_slot = rows_y * per_part
    capacity = pair_list.shape[4]
    fill = block_fill.reshape(blocks)
    count = pair_count.reshape(1)
    limit = 24 << 20

    x0, packed = call(
        pack_kernel,
        (jax.ShapeDtypeStruct(shape, f32), jax.ShapeDtypeStruct((blocks, samples + 8, width), bf16)),
        [SMEM, VMEM, VMEM],
    )(fill, noise.reshape(shape), positions.reshape(blocks, 3, beads))
    table = pair_table(pair_list, pair_count, blocks, columns, zero_slot)
    out_field = (jax.ShapeDtypeStruct(shape, f32), jax.ShapeDtypeStruct(shape, bf16))

    def scratch(rows):
        return (pltpu.VMEM((zero_slot + 1, rows, width), bf16), pltpu.VMEM(shape, f32))

    parts = spread(packed)
    tiles, x1, send = call(
        functools.partial(first_kernel, rows_y, 0, beads),
        (jax.ShapeDtypeStruct((capacity, width, width), bf16),) + out_field,
        [SMEM] * 3 + [VMEM] * (1 + rows_y),
        scratch(samples + 8),
        limit,
    )(count, fill, table, x0, *parts)
    parts = spread(send)
    x2, send = call(
        functools.partial(next_kernel, rows_y, beads),
        out_field,
        [SMEM] * 3 + [VMEM] * (2 + rows_y),
        scratch(samples),
        limit,
    )(count, fill, table, tiles, x1, *parts)
    parts = spread(send)
    moments = call(
        functools.partial(last_kernel, rows_y, beads),
        jax.ShapeDtypeStruct((devices, 1, 128), f32),
        [SMEM] * 3 + [VMEM] * (4 + rows_y),
        scratch(samples),
        limit,
    )(count, fill, table, tiles, x0, x1, x2, *parts)
    moments = lax.all_to_all(moments, AXES, 0, 0)
    out = call(final_kernel, jax.ShapeDtypeStruct(shape, f32), [VMEM] * 4)(moments, x0, x1, x2)
    return out.reshape(noise.shape)


def solution(mesh):
    block = P("gx", "gy", "gz", None, None)
    cell = P("gx", "gy", "gz")
    return jax.shard_map(
        body, mesh=mesh, in_specs=(block, cell, block, block, cell), out_specs=block, check_vma=False
    )
```

```python
import functools

import jax
import jax.numpy as jnp
from jax import lax
from jax.experimental import pallas as pl
from jax.experimental.pallas import tpu as pltpu
from jax.sharding import PartitionSpec as P

ITERS = 3
ROOT_ITERS = 12
GROUP = 4
CHUNK = 32

radius = 0.08
floor_sq = 0.0001
epsilon = 1e-06

AXES = ("gx", "gy", "gz")
VMEM = pl.BlockSpec(memory_space=pltpu.VMEM)
HBM = pl.BlockSpec(memory_space=pltpu.HBM)
SMEM = pl.BlockSpec(memory_space=pltpu.SMEM)
f32 = jnp.float32
bf16 = jnp.bfloat16
PLACES = ((0, 0), (0, 1), (0, 2), (1, 1), (1, 2), (2, 2))


def matching(count, parity):
    pairs = []
    for i in range(parity, count - 1, 2):
        pairs += [(i, i + 1), (i + 1, i)]
    return pairs


def swaps(axis, first, second):
    count = lax.axis_size(axis)
    got = [lax.ppermute(first, axis, matching(count, 0))]
    if count > 2:
        got.append(lax.ppermute(second, axis, matching(count, 1)))
    return got


def spread(field):
    blocks, rows, width = field.shape
    columns = jnp.stack([field] + swaps("gx", field, field))
    odd = lax.axis_index("gz") % 2 == 1
    low, high = columns[:, 0], columns[:, blocks - 1]
    got = swaps("gz", jnp.where(odd, low, high), jnp.where(odd, high, low))
    while len(got) < 2:
        got.append(jnp.zeros_like(got[0]))
    deep = jnp.concatenate([columns] + [g[:, None] for g in got], axis=1)
    deep = deep.reshape(-1, rows, width)
    return [deep] + swaps("gy", deep, deep)


def partner(axis, step):
    if lax.axis_size(axis) == 2:
        return jnp.where(step == 0, 0, 1)
    odd = lax.axis_index(axis) % 2
    return jnp.where(step == 0, 0, jnp.where((step < 0) == (odd == 1), 1, 2))


def pair_table(pair_list, pair_count, blocks, columns, zero_slot):
    home, code = pair_list[0, 0, 0, 0], pair_list[0, 0, 0, 1]
    capacity = home.shape[0]
    size = -(-(capacity + blocks * (GROUP - 1)) // GROUP + 1) * GROUP
    step_x, step_y, step_z = code // 9 - 1, code // 3 % 3 - 1, code % 3 - 1
    z = home + step_z
    odd = lax.axis_index("gz") % 2
    below = jnp.where(odd == 1, blocks, blocks + 1)
    above = jnp.where(odd == 1, blocks + 1, blocks)
    if lax.axis_size("gz") == 2:
        below = above = blocks
    z = jnp.where(z < 0, below, jnp.where(z >= blocks, above, z))
    slot = (partner("gy", step_y) * columns + partner("gx", step_x)) * (blocks + 2) + z
    order = lax.iota(jnp.int32, capacity)
    live = order < pair_count[0, 0, 0]
    earlier = order[None, :] < order[:, None]
    place = jnp.zeros_like(order)
    starts = []
    start = jnp.zeros((), jnp.int32)
    index = lax.iota(jnp.int32, size)
    for block in range(blocks):
        mine = live & (home == block)
        rank = jnp.sum(jnp.where(earlier & mine[None, :], 1, 0), axis=1)
        starts.append(start)
        place = jnp.where(mine, start + rank, place)
        start = start + (jnp.sum(jnp.where(mine, 1, 0)) + GROUP - 1) // GROUP * GROUP
    there = live[:, None] & (place[:, None] == index[None, :])
    slots = jnp.sum(jnp.where(there, slot[:, None] - zero_slot, 0), axis=0) + zero_slot
    homes = sum(jnp.where(index * GROUP >= first, 1, 0) for first in starts) - 1
    groups = jnp.full((size,), start // GROUP, jnp.int32)
    return jnp.stack([slots, homes, groups])


def pack_kernel(fill_hbm, noise_hbm, pos_hbm, start_ref, mask_ref, pack_ref, fill_ref, noise_ref, pos_ref, sems):
    pairs = ((fill_hbm, fill_ref), (noise_hbm, noise_ref), (pos_hbm, pos_ref))
    copies = [pltpu.make_async_copy(a, b, sems.at[i]) for i, (a, b) in enumerate(pairs)]
    for copy in copies:
        copy.start()
    for copy in copies:
        copy.wait()
    blocks, samples, width = noise_ref.shape[2:]
    beads = width // 3
    row = lax.broadcasted_iota(jnp.int32, (16, beads), 0)
    for block in range(blocks):
        mask = (lax.broadcasted_iota(jnp.int32, (8, beads), 1) < fill_ref[0, 0, block]).astype(f32)
        mask_ref[block] = mask
        noise = [noise_ref[0, 0, block, :, pl.ds(c * beads, beads)] for c in range(3)]
        start = jnp.concatenate([part * mask[:1] for part in noise], axis=0)
        start_ref[block] = start
        place = jnp.zeros((16, beads), f32)
        for c in range(3):
            pos = pos_ref[0, 0, c, pl.ds(block, 1)]
            high = pos.astype(bf16).astype(f32)
            rest = pos - high
            mid = rest.astype(bf16).astype(f32)
            for i, piece in enumerate((high, mid, rest - mid)):
                place = jnp.where(row == 3 * i + c, piece, place)
        pack_ref[block] = jnp.concatenate([start, place], axis=0).astype(bf16)


def gather_slots(parts, slots_ref):
    count = parts[0].shape[0]
    for i, part in enumerate(parts):
        slots_ref[pl.ds(i * count, count)] = part[...]
    slots_ref[len(parts) * count] = jnp.zeros(slots_ref.shape[1:], bf16)


def position_of(slots_ref, slot, field_rows):
    rows = slots_ref[slot].astype(f32)[field_rows:]
    return [rows[c : c + 1] + rows[3 + c : 4 + c] + rows[6 + c : 7 + c] for c in range(3)]


def turn_position(slots_ref, slot, field_rows):
    away = position_of(slots_ref, slot, field_rows)
    row = lax.broadcasted_iota(jnp.int32, (8, away[0].shape[1]), 0)
    return jnp.transpose(jnp.where(row == 0, away[0], jnp.where(row == 1, away[1], away[2])))


def make_tile(home, turned_ref, tiles_ref, pair, base):
    beads = home[0].shape[1]
    for first in range(0, beads, CHUNK):
        turned = turned_ref[pl.ds(first, CHUNK)]
        d = [turned[:, c : c + 1] - home[c] for c in range(3)]
        dist_sq = d[0] * d[0] + d[1] * d[1] + d[2] * d[2]
        root = lax.rsqrt(jnp.maximum(dist_sq, 1e-30))
        distance = dist_sq * root
        inv_root = jnp.minimum(root, floor_sq**-0.5)
        inverse_sq = inv_root * inv_root
        far = (0.75 * radius) * inv_root
        far_two = (2.0 * radius * radius) * (far * inverse_sq)
        apart = dist_sq >= 4.0 * radius * radius
        isotropic = jnp.where(apart, far + far_two * (1.0 / 3.0), 1.0 - (9.0 / 32.0 / radius) * distance)
        dyadic = jnp.where(apart, far - far_two, (3.0 / 32.0 / radius) * distance) * inverse_sq
        scaled = [dyadic * d[c] for c in range(3)]
        for k, (c, e) in enumerate(PLACES):
            entry = scaled[c] * d[e]
            if c == e:
                entry = entry + isotropic
            tiles_ref[pair, pl.ds(base + first, CHUNK), pl.ds(k * beads, beads)] = entry.astype(bf16)


def add_product(sum_ref, home, product):
    rows, beads = sum_ref.shape[1:]
    samples = rows // 3
    out = [0.0] * 3
    for k, (c, e) in enumerate(PLACES):
        column = product[:, k * beads : (k + 1) * beads]
        out[c] = out[c] + column[e * samples : (e + 1) * samples]
        if c != e:
            out[e] = out[e] + column[c * samples : (c + 1) * samples]
    sum_ref[home] = sum_ref[home] + jnp.concatenate(out, axis=0)


def field_of(table_ref, slots_ref, first, rows):
    return jnp.concatenate([slots_ref[table_ref[0, first + i]][:rows] for i in range(2)], axis=1)


def multiply(table_ref, slots_ref, even_ref, odd_ref, sum_ref, zero_slot):
    rows = sum_ref.shape[1]
    sum_ref[...] = jnp.zeros_like(sum_ref)

    def group(turn, carry):
        first = turn * GROUP
        field = [field_of(table_ref, slots_ref, first + i, rows) for i in (0, 2)]
        odd = jnp.where(table_ref[0, first + 2] == zero_slot, 0, turn)
        tile = jnp.concatenate([even_ref[turn], odd_ref[odd]], axis=0)
        product = jnp.dot(jnp.concatenate(field, axis=1), tile, preferred_element_type=f32)
        add_product(sum_ref, table_ref[1, turn], product)
        return carry

    lax.fori_loop(0, table_ref[2, 0], group, 0)


def new_field(block, mask_ref, sum_ref, old_ref):
    return sum_ref[block] * mask_ref[block, :1] - old_ref[block]


def first_kernel(parts, zero_slot, table_ref, mask_ref, start_ref, *refs):
    given, refs = refs[:parts], refs[parts:]
    even_ref, odd_ref, next_ref, send_ref, slots_ref, sum_ref, turn_even, turn_odd = refs
    blocks, rows, beads = start_ref.shape
    gather_slots(given, slots_ref)
    sum_ref[...] = jnp.zeros_like(sum_ref)
    odd_ref[0] = jnp.zeros(odd_ref.shape[1:], bf16)

    def prepare(first, turned_ref):
        for i in range(2):
            turned_ref[i, :, :8] = turn_position(slots_ref, table_ref[0, first + i], rows)

    def consume(first, tile, index):
        product = jnp.dot(
            field_of(table_ref, slots_ref, first, rows), tile[index], preferred_element_type=f32
        )
        add_product(sum_ref, table_ref[1, first // GROUP], product)

    def make(home, turned_ref, tile, index):
        for i in range(2):
            make_tile(home, turned_ref.at[i], tile, index, i * beads)

    def group(turn, carry):
        pending, spare = carry
        first = turn * GROUP
        home = position_of(slots_ref, table_ref[1, turn], rows)
        full = table_ref[0, first + 2] != zero_slot
        prepare(first + 2, turn_odd)
        consume(pending, odd_ref, spare)
        make(home, turn_even, even_ref, turn)

        @pl.when(full)
        def _():
            prepare(first + GROUP, turn_even)
            consume(first, even_ref, turn)
            make(home, turn_odd, odd_ref, turn)

        @pl.when(jnp.logical_not(full))
        def _():
            prepare(first + GROUP, turn_even)
            consume(first, even_ref, turn)

        return first + 2, jnp.where(full, turn, spare)

    prepare(0, turn_even)
    none = table_ref.shape[1] - 2
    pending, spare = lax.fori_loop(0, table_ref[2, 0], group, (none, 0))
    consume(pending, odd_ref, spare)
    for block in range(blocks):
        new = new_field(block, mask_ref, sum_ref, start_ref)
        next_ref[block] = new
        send_ref[block] = new.astype(bf16)


def next_kernel(parts, zero_slot, table_ref, mask_ref, even_ref, odd_ref, old_ref, *refs):
    given, (next_ref, send_ref, slots_ref, sum_ref) = refs[:parts], refs[parts:]
    gather_slots(given, slots_ref)
    multiply(table_ref, slots_ref, even_ref, odd_ref, sum_ref, zero_slot)
    for block in range(old_ref.shape[0]):
        new = new_field(block, mask_ref, sum_ref, old_ref)
        next_ref[block] = new
        send_ref[block] = new.astype(bf16)


MOMENTS = ((0, 0), (0, 1), (1, 1), (1, 2), (2, 2), (2, 3))


def last_kernel(parts, zero_slot, table_ref, mask_ref, even_ref, odd_ref, x0_ref, x1_ref, x2_ref, *refs):
    given, (moment_ref, slots_ref, sum_ref) = refs[:parts], refs[parts:]
    blocks, rows, beads = x0_ref.shape
    samples = rows // 3
    gather_slots(given, slots_ref)
    multiply(table_ref, slots_ref, even_ref, odd_ref, sum_ref, zero_slot)
    lanes = moment_ref.shape[2]
    lane = lax.broadcasted_iota(jnp.int32, (samples, lanes), 1)
    row = lax.broadcasted_iota(jnp.int32, (samples, lanes), 0)
    sums = [0.0] * len(MOMENTS)
    for block in range(blocks):
        x = [x0_ref[block], x1_ref[block], x2_ref[block]]
        x.append(new_field(block, mask_ref, sum_ref, x2_ref))
        for k, (i, j) in enumerate(MOMENTS):
            both = x[i] * x[j]
            sums[k] = sums[k] + both[:samples] + both[samples : 2 * samples] + both[2 * samples :]
    grid = jnp.zeros((samples, lanes), f32)
    for k, value in enumerate(sums):
        value = jnp.sum(value, axis=1, keepdims=True)
        grid = jnp.where(lane == row + k * samples, value, grid)
    line = jnp.sum(grid, axis=0, keepdims=True)
    moment_ref[...] = jnp.broadcast_to(line[None], moment_ref.shape)


def inverse_symmetric(m):
    a, b, c, d, e, f = m
    ca, cb, cc = d * f - e * e, c * e - b * f, b * e - c * d
    scale = 1.0 / (a * ca + b * cb + c * cc)
    return (ca * scale, cb * scale, cc * scale, (a * f - c * c) * scale, (b * c - a * e) * scale, (a * d - b * b) * scale)


def final_kernel(moment_ref, x0_ref, x1_ref, x2_ref, out_ref):
    blocks, rows, beads = x0_ref.shape
    samples = rows // 3
    lanes = moment_ref.shape[2]
    lane = lax.broadcasted_iota(jnp.int32, (samples, lanes), 1)
    row = lax.broadcasted_iota(jnp.int32, (samples, lanes), 0)
    line = jnp.broadcast_to(jnp.sum(moment_ref[...], axis=0), (samples, lanes))
    m00, m01, m11, m12, m22, m23 = [
        jnp.broadcast_to(
            jnp.sum(jnp.where(lane == row + k * samples, line, 0.0), axis=1, keepdims=True), (samples, lanes)
        )
        for k in range(len(MOMENTS))
    ]
    norm_sq = m00 + epsilon
    start_norm = jnp.sqrt(norm_sq)
    inv_sq = 1.0 / norm_sq
    alpha1 = (m00 + m01) * inv_sq
    c = 1.0 - alpha1
    res_sq = (m11 + c * (2.0 * m01 + c * m00)) * inv_sq
    beta1 = jnp.sqrt(jnp.maximum(res_sq, 0.0) + epsilon)
    k2 = 1.0 / (start_norm * beta1)
    n11 = m11 + c * (2.0 * m01 + c * m00)
    n12 = m12 + c * (2.0 * m11 + c * m01)
    alpha2 = k2 * k2 * (n11 + n12)
    f1 = 1.0 + c - alpha2
    f0 = c - alpha2 * c - beta1 * beta1
    n22 = m22 + f1 * (2.0 * m12 + f1 * m11) + f0 * (2.0 * (m11 + f1 * m01) + f0 * m00)
    beta2 = jnp.sqrt(jnp.maximum(k2 * k2 * n22, 0.0) + epsilon)
    k3 = k2 / beta2
    n23 = m23 + f1 * (2.0 * m22 + f1 * m12) + f0 * (2.0 * (m12 + f1 * m11) + f0 * m01)
    alpha3 = k3 * k3 * (jnp.maximum(n22, 0.0) + n23)

    scale = (alpha1 + alpha2 + alpha3) / 3.0
    inv_scale = 1.0 / scale
    zero, one = jnp.zeros_like(scale), jnp.ones_like(scale)
    y = (alpha1 * inv_scale, beta1 * inv_scale, zero, alpha2 * inv_scale, beta2 * inv_scale, alpha3 * inv_scale)
    z = (one, zero, zero, one, zero, one)
    for _ in range(ROOT_ITERS):
        inv_z, inv_y = inverse_symmetric(z), inverse_symmetric(y)
        y = tuple(0.5 * (p + q) for p, q in zip(y, inv_z))
        z = tuple(0.5 * (p + q) for p, q in zip(z, inv_y))
    root_scale = jnp.sqrt(scale)
    r1, r2, r3 = root_scale * y[0], root_scale * y[1], root_scale * y[2]
    w2, w3 = start_norm * r2 * k2, start_norm * r3 * k3
    p0 = r1 + w2 * c + w3 * f0
    p1 = w2 + w3 * f1
    for block in range(blocks):
        for c in range(3):
            at = pl.ds(c * samples, samples)
            out = p0 * x0_ref[block, at] + p1 * x1_ref[block, at] + w3 * x2_ref[block, at]
            out_ref[0, 0, block, :, pl.ds(c * beads, beads)] = out


def call(kernel, outs, in_specs, scratch=(), limit=None, cost=None):
    return pl.pallas_call(
        kernel,
        out_shape=outs,
        in_specs=in_specs,
        out_specs=jax.tree.map(lambda _: VMEM, outs),
        scratch_shapes=list(scratch),
        compiler_params=pltpu.CompilerParams(vmem_limit_bytes=limit),
        cost_estimate=cost,
    )


def body(positions, block_fill, noise, pair_list, pair_count):
    blocks, beads = positions.shape[2], positions.shape[4]
    samples = noise.shape[3]
    rows = 3 * samples
    shape = (blocks, rows, beads)
    devices = lax.axis_size(AXES)
    columns = 2 if lax.axis_size("gx") == 2 else 3
    parts_y = 2 if lax.axis_size("gy") == 2 else 3
    zero_slot = parts_y * columns * (blocks + 2)
    limit = 24 << 20

    x0, mask, packed = call(
        pack_kernel,
        (
            jax.ShapeDtypeStruct(shape, f32),
            jax.ShapeDtypeStruct((blocks, 8, beads), f32),
            jax.ShapeDtypeStruct((blocks, rows + 16, beads), bf16),
        ),
        [HBM] * 3,
        (
            pltpu.SMEM(block_fill.shape, jnp.int32),
            pltpu.VMEM(noise.shape, f32),
            pltpu.VMEM((1, 1, 3, blocks, beads), f32),
            pltpu.SemaphoreType.DMA((3,)),
        ),
        4 << 20,
    )(block_fill, noise, jnp.swapaxes(positions, 2, 3))
    table = pair_table(pair_list, pair_count, blocks, columns, zero_slot)
    out_field = (jax.ShapeDtypeStruct(shape, f32), jax.ShapeDtypeStruct(shape, bf16))
    tile = jax.ShapeDtypeStruct((table.shape[1] // GROUP, 2 * beads, len(PLACES) * beads), bf16)

    def scratch(rows):
        return (pltpu.VMEM((zero_slot + 1, rows, beads), bf16), pltpu.VMEM(shape, f32))

    parts = spread(packed)
    even, odd, x1, send = call(
        functools.partial(first_kernel, parts_y, zero_slot),
        (tile, tile) + out_field,
        [SMEM] + [VMEM] * (2 + parts_y),
        scratch(rows + 16) + (pltpu.VMEM((2, beads, 128), f32),) * 2,
        limit,
    )(table, mask, x0, *parts)
    parts = spread(send)
    x2, send = call(
        functools.partial(next_kernel, parts_y, zero_slot),
        out_field,
        [SMEM] + [VMEM] * (4 + parts_y),
        scratch(rows),
        limit,
    )(table, mask, even, odd, x1, *parts)
    parts = spread(send)
    moments = call(
        functools.partial(last_kernel, parts_y, zero_slot),
        jax.ShapeDtypeStruct((devices, 1, 128), f32),
        [SMEM] + [VMEM] * (6 + parts_y),
        scratch(rows),
        limit,
    )(table, mask, even, odd, x0, x1, x2, *parts)
    moments = lax.all_to_all(moments, AXES, 0, 0)
    return call(final_kernel, jax.ShapeDtypeStruct(noise.shape, f32), [VMEM] * 4, (), 4 << 20)(moments, x0, x1, x2)


def solution(mesh):
    block = P("gx", "gy", "gz", None, None)
    cell = P("gx", "gy", "gz")
    return jax.shard_map(
        body, mesh=mesh, in_specs=(block, cell, block, block, cell), out_specs=block, check_vma=False
    )
```

```python
import functools

import jax
import jax.numpy as jnp
from jax import lax
from jax.experimental import pallas as pl
from jax.experimental.pallas import tpu as pltpu
from jax.sharding import PartitionSpec as P

ITERS = 3
ROOT_ITERS = 12
GROUP = 4
CHUNK = 32

radius = 0.08
floor_sq = 0.0001
epsilon = 1e-06

AXES = ("gx", "gy", "gz")
VMEM = pl.BlockSpec(memory_space=pltpu.VMEM)
HBM = pl.BlockSpec(memory_space=pltpu.HBM)
SMEM = pl.BlockSpec(memory_space=pltpu.SMEM)
f32 = jnp.float32
bf16 = jnp.bfloat16
PLACES = ((0, 0), (0, 1), (0, 2), (1, 1), (1, 2), (2, 2))


def matching(count, parity):
    pairs = []
    for i in range(parity, count - 1, 2):
        pairs += [(i, i + 1), (i + 1, i)]
    return pairs


def swaps(axis, first, second):
    count = lax.axis_size(axis)
    got = [lax.ppermute(first, axis, matching(count, 0))]
    if count > 2:
        got.append(lax.ppermute(second, axis, matching(count, 1)))
    return got


def spread(field, *before):
    columns = jnp.stack([field] + swaps("gx", field, field))
    columns, *before = lax.optimization_barrier((columns, *before))
    columns = jnp.concatenate([columns] + swaps("gy", columns, columns))
    odd = lax.axis_index("gz") % 2 == 1
    low, high = columns[:, 0], columns[:, field.shape[0] - 1]
    far = swaps("gz", jnp.where(odd, low, high), jnp.where(odd, high, low))
    return columns.reshape((-1,) + field.shape[1:]), far, *before


def table_kernel(sizes, slots, blocks, odd_ref, count_ref, list_hbm, near_ref, far_ref, list_ref, sem):
    copy = pltpu.make_async_copy(list_hbm, list_ref, sem)
    copy.start()
    outs = (near_ref, far_ref)
    for out, empty in zip(outs, slots):
        for block in range(blocks):
            out[1, block] = 0
        for i in range(2):
            out[0, out.shape[1] - 1 - i] = empty
    odd = [odd_ref[axis] == 1 for axis in range(3)]

    def partner(axis, step):
        if sizes[axis] == 2:
            return jnp.where(step == 0, 0, 1)
        return jnp.where(step == 0, 0, jnp.where((step < 0) == odd[axis], 1, 2))

    segment = near_ref.shape[1] // blocks

    def enter(t, carry):
        home, code = list_ref[0, 0, 0, 0, t], list_ref[0, 0, 1, 0, t]
        plane, third = (code * 57) >> 9, (code * 43) >> 7
        column = partner(1, third - 3 * plane - 1) * (2 if sizes[0] == 2 else 3) + partner(0, plane - 1)
        z = home + code - 3 * third - 1
        far = (z < 0) | (z >= blocks)

        @pl.when(jnp.logical_not(far))
        def _():
            place = near_ref[1, home]
            near_ref[1, home] = place + 1
            near_ref[0, home * segment + place] = column * blocks + z

        @pl.when(far)
        def _():
            place = far_ref[1, home]
            far_ref[1, home] = place + 1
            side = partner(2, jnp.where(z < 0, -1, 1)) - 1
            far_ref[0, home * segment + place] = side * (slots[0] // blocks) + column

        return carry

    copy.wait()
    lax.fori_loop(0, count_ref[0, 0, 0], enter, 0)
    for out, empty in zip(outs, slots):
        for block in range(blocks):
            end = block * segment + out[1, block]
            for i in range(GROUP + 1):
                out[0, end + i] = empty


def pair_tables(pair_list, pair_count, blocks, near_slots, far_slots):
    segment = -(-pair_list.shape[4] // GROUP + 2) * GROUP
    table = jax.ShapeDtypeStruct((2, blocks * segment), jnp.int32)
    sizes = [lax.axis_size(axis) for axis in AXES]
    odd = jnp.stack([lax.axis_index(axis) % 2 for axis in AXES])
    pair_list = pltpu.with_memory_space_constraint(jnp.swapaxes(pair_list, 2, 3), pltpu.HBM)
    return pl.pallas_call(
        functools.partial(table_kernel, sizes, (near_slots, far_slots), blocks),
        out_shape=(table, table),
        in_specs=[SMEM, SMEM, HBM],
        out_specs=(SMEM, SMEM),
        scratch_shapes=[
            pltpu.SMEM(pair_list.shape, jnp.int32),
            pltpu.SemaphoreType.DMA,
        ],
        compiler_params=pltpu.CompilerParams(vmem_limit_bytes=1 << 20),
        cost_estimate=pl.CostEstimate(flops=10**6, bytes_accessed=10**6, transcendentals=0),
    )(odd, pair_count, pair_list)


def groups_of(table_ref, blocks):
    segment = table_ref.shape[1] // blocks
    counts = [(table_ref[1, block] + (GROUP - 1)) // GROUP for block in range(blocks)]
    ends = [sum(counts[: block + 1]) for block in range(blocks)]

    def home_of(turn):
        return sum([jnp.where(turn >= end, 1, 0) for end in ends[:-1]], 0)

    def first_of(turn):
        skip = [jnp.where(turn >= ends[i], segment - counts[i] * GROUP, 0) for i in range(blocks - 1)]
        return turn * GROUP + sum(skip)

    return ends[-1], home_of, first_of


def pack_kernel(fill_hbm, noise_hbm, pos_hbm, start_ref, mask_ref, pack_ref, fill_ref, noise_ref, pos_ref, sems):
    pairs = ((fill_hbm, fill_ref), (noise_hbm, noise_ref), (pos_hbm, pos_ref))
    copies = [pltpu.make_async_copy(a, b, sems.at[i]) for i, (a, b) in enumerate(pairs)]
    for copy in copies:
        copy.start()
    for copy in copies:
        copy.wait()
    blocks, samples, width = noise_ref.shape[2:]
    beads = width // 3
    row = lax.broadcasted_iota(jnp.int32, (16, beads), 0)
    for block in range(blocks):
        mask = (lax.broadcasted_iota(jnp.int32, (8, beads), 1) < fill_ref[0, 0, block]).astype(f32)
        mask_ref[block] = mask
        noise = [noise_ref[0, 0, block, :, pl.ds(c * beads, beads)] for c in range(3)]
        start = jnp.concatenate([part * mask[:1] for part in noise], axis=0)
        start_ref[block] = start
        place = jnp.zeros((16, beads), f32)
        for c in range(3):
            pos = pos_ref[0, 0, c, pl.ds(block, 1)]
            high = pos.astype(bf16).astype(f32)
            rest = pos - high
            mid = rest.astype(bf16).astype(f32)
            for i, piece in ((0, high), (8, mid), (3, rest - mid)):
                place = jnp.where(row == i + c, piece, place)
        pack_ref[block] = jnp.concatenate([start, place], axis=0).astype(bf16)


def gather_slots(parts, slots_ref):
    count = parts[0].shape[0]
    for i, part in enumerate(parts):
        slots_ref[pl.ds(i * count, count)] = part[...]
    slots_ref[len(parts) * count] = jnp.zeros(slots_ref.shape[1:], bf16)


def position_of(slots_ref, slot, field_rows):
    rows = slots_ref[slot].astype(f32)[field_rows:]
    return rows[:8] + rows[8:] + pltpu.roll(rows[:8], 5, 0)


def turn_positions(slots_ref, first, second, field_rows):
    first = position_of(slots_ref, first, field_rows)
    second = pltpu.roll(position_of(slots_ref, second, field_rows), 3, 0)
    row = lax.broadcasted_iota(jnp.int32, first.shape, 0)
    return jnp.transpose(jnp.where(row < 3, first, second))


def make_tile(home, turned_ref, tiles_ref, pair, half):
    beads = home.shape[1]
    base = half * beads
    for first in range(0, beads, CHUNK):
        turned = turned_ref[pl.ds(first, CHUNK)]
        d = [turned[:, 3 * half + c : 3 * half + c + 1] - home[c : c + 1] for c in range(3)]
        dist_sq = d[0] * d[0] + d[1] * d[1] + d[2] * d[2]
        root = lax.rsqrt(jnp.maximum(dist_sq, 1e-30))
        distance = dist_sq * root
        inv_root = jnp.minimum(root, floor_sq**-0.5)
        inverse_sq = inv_root * inv_root
        far = (0.75 * radius) * inv_root
        far_two = (2.0 * radius * radius) * (far * inverse_sq)
        apart = dist_sq >= 4.0 * radius * radius
        isotropic = jnp.where(apart, far + far_two * (1.0 / 3.0), 1.0 - (9.0 / 32.0 / radius) * distance)
        dyadic = jnp.where(apart, far - far_two, (3.0 / 32.0 / radius) * distance) * inverse_sq
        scaled = [dyadic * d[c] for c in range(3)]
        for k, (c, e) in enumerate(PLACES):
            entry = scaled[c] * d[e]
            if c == e:
                entry = entry + isotropic
            tiles_ref[pair, pl.ds(base + first, CHUNK), pl.ds(k * beads, beads)] = entry.astype(bf16)


def add_product(sum_ref, home, product):
    rows, beads = sum_ref.shape[1:]
    samples = rows // 3
    out = [0.0] * 3
    for k, (c, e) in enumerate(PLACES):
        column = product[:, k * beads : (k + 1) * beads]
        out[c] = out[c] + column[e * samples : (e + 1) * samples]
        if c != e:
            out[e] = out[e] + column[c * samples : (c + 1) * samples]
    sum_ref[home] = sum_ref[home] + jnp.concatenate(out, axis=0)


def field_of(table_ref, slots_ref, first, rows):
    return jnp.concatenate([slots_ref[table_ref[0, first + i]][:rows] for i in range(2)], axis=1)


def multiply(table_ref, slots_ref, even_ref, odd_ref, sum_ref):
    blocks, rows = sum_ref.shape[:2]
    zero_slot = slots_ref.shape[0] - 1
    count, home_of, first_of = groups_of(table_ref, blocks)

    def group(turn, carry):
        first = first_of(turn)
        field = [field_of(table_ref, slots_ref, first + i, rows) for i in (0, 2)]
        odd = jnp.where(table_ref[0, first + 2] == zero_slot, 0, turn)
        tile = jnp.concatenate([even_ref[turn], odd_ref[odd]], axis=0)
        product = jnp.dot(jnp.concatenate(field, axis=1), tile, preferred_element_type=f32)
        add_product(sum_ref, home_of(turn), product)
        return carry

    lax.fori_loop(0, count, group, 0)


def new_field(block, mask_ref, sum_ref, old_ref):
    return sum_ref[block] * mask_ref[block, :1] - old_ref[block]


def build(table_ref, own_ref, slots_ref, even_ref, odd_ref, sum_ref, turn_even, turn_odd):
    blocks, rows, beads = sum_ref.shape
    zero_slot = slots_ref.shape[0] - 1
    count, home_of, first_of = groups_of(table_ref, blocks)
    odd_ref[0] = jnp.zeros(odd_ref.shape[1:], bf16)

    def prepare(first, turned_ref):
        turned_ref[:, :8] = turn_positions(slots_ref, table_ref[0, first], table_ref[0, first + 1], rows)

    def consume(home, first, tile, index):
        product = jnp.dot(
            field_of(table_ref, slots_ref, first, rows), tile[index], preferred_element_type=f32
        )
        add_product(sum_ref, home, product)

    def make(home, turned_ref, tile, index):
        for i in range(2):
            make_tile(home, turned_ref, tile, index, i)

    def group(turn, carry):
        pending, pending_home, spare = carry
        first, home = first_of(turn), home_of(turn)
        place = position_of(own_ref, home, rows)
        full = table_ref[0, first + 2] != zero_slot
        make(place, turn_even, even_ref, turn)
        prepare(first + 2, turn_odd)
        consume(pending_home, pending, odd_ref, spare)

        @pl.when(full)
        def _():
            make(place, turn_odd, odd_ref, turn)
            prepare(first_of(turn + 1), turn_even)
            consume(home, first, even_ref, turn)

        @pl.when(jnp.logical_not(full))
        def _():
            prepare(first_of(turn + 1), turn_even)
            consume(home, first, even_ref, turn)

        return first + 2, home, jnp.where(full, turn, spare)

    prepare(first_of(0), turn_even)
    none = table_ref.shape[1] - 2
    pending, pending_home, spare = lax.fori_loop(0, count, group, (none, 0, 0))
    consume(pending_home, pending, odd_ref, spare)


def build_near(table_ref, own_ref, part_ref, even_ref, odd_ref, sum_ref, slots_ref, *turned):
    gather_slots([part_ref], slots_ref)
    sum_ref[...] = jnp.zeros_like(sum_ref)
    build(table_ref, own_ref, slots_ref, even_ref, odd_ref, sum_ref, *turned)


def build_far(sides, table_ref, own_ref, mask_ref, old_ref, near_ref, *refs):
    given, (even_ref, odd_ref, next_ref, send_ref, slots_ref, sum_ref, *turned) = refs[:sides], refs[sides:]
    gather_slots(given, slots_ref)
    sum_ref[...] = near_ref[...]
    build(table_ref, own_ref, slots_ref, even_ref, odd_ref, sum_ref, *turned)
    finish(mask_ref, sum_ref, old_ref, next_ref, send_ref)


def apply_near(table_ref, even_ref, odd_ref, part_ref, sum_ref, slots_ref):
    gather_slots([part_ref], slots_ref)
    sum_ref[...] = jnp.zeros_like(sum_ref)
    multiply(table_ref, slots_ref, even_ref, odd_ref, sum_ref)


def apply_far(sides, table_ref, even_ref, odd_ref, mask_ref, old_ref, near_ref, *refs):
    given, (next_ref, send_ref, slots_ref, sum_ref) = refs[:sides], refs[sides:]
    gather_slots(given, slots_ref)
    sum_ref[...] = near_ref[...]
    multiply(table_ref, slots_ref, even_ref, odd_ref, sum_ref)
    finish(mask_ref, sum_ref, old_ref, next_ref, send_ref)


def finish(mask_ref, sum_ref, old_ref, next_ref, send_ref):
    for block in range(old_ref.shape[0]):
        new = new_field(block, mask_ref, sum_ref, old_ref)
        next_ref[block] = new
        send_ref[block] = new.astype(bf16)


MOMENTS = ((0, 0), (0, 1), (1, 1), (1, 2), (2, 2), (2, 3))


def last_far(sides, table_ref, even_ref, odd_ref, mask_ref, x0_ref, x1_ref, x2_ref, near_ref, *refs):
    given, (moment_ref, slots_ref, sum_ref) = refs[:sides], refs[sides:]
    blocks, rows, beads = x0_ref.shape
    samples = rows // 3
    gather_slots(given, slots_ref)
    sum_ref[...] = near_ref[...]
    multiply(table_ref, slots_ref, even_ref, odd_ref, sum_ref)
    lanes = moment_ref.shape[2]
    lane = lax.broadcasted_iota(jnp.int32, (samples, lanes), 1)
    row = lax.broadcasted_iota(jnp.int32, (samples, lanes), 0)
    sums = [0.0] * len(MOMENTS)
    for block in range(blocks):
        x = [x0_ref[block], x1_ref[block], x2_ref[block]]
        x.append(new_field(block, mask_ref, sum_ref, x2_ref))
        for k, (i, j) in enumerate(MOMENTS):
            both = x[i] * x[j]
            sums[k] = sums[k] + both[:samples] + both[samples : 2 * samples] + both[2 * samples :]
    grid = jnp.zeros((samples, lanes), f32)
    for k, value in enumerate(sums):
        value = jnp.sum(value, axis=1, keepdims=True)
        grid = jnp.where(lane == row + k * samples, value, grid)
    line = jnp.sum(grid, axis=0, keepdims=True)
    moment_ref[...] = jnp.broadcast_to(line[None], moment_ref.shape)


def inverse_symmetric(m):
    a, b, c, d, e, f = m
    ca, cb, cc = d * f - e * e, c * e - b * f, b * e - c * d
    scale = 1.0 / (a * ca + b * cb + c * cc)
    return (ca * scale, cb * scale, cc * scale, (a * f - c * c) * scale, (b * c - a * e) * scale, (a * d - b * b) * scale)


def final_kernel(moment_ref, x0_ref, x1_ref, x2_ref, out_ref):
    blocks, rows, beads = x0_ref.shape
    samples = rows // 3
    lanes = moment_ref.shape[2]
    lane = lax.broadcasted_iota(jnp.int32, (samples, lanes), 1)
    row = lax.broadcasted_iota(jnp.int32, (samples, lanes), 0)
    line = jnp.broadcast_to(jnp.sum(moment_ref[...], axis=0), (samples, lanes))
    m00, m01, m11, m12, m22, m23 = [
        jnp.broadcast_to(
            jnp.sum(jnp.where(lane == row + k * samples, line, 0.0), axis=1, keepdims=True), (samples, lanes)
        )
        for k in range(len(MOMENTS))
    ]
    norm_sq = m00 + epsilon
    start_norm = jnp.sqrt(norm_sq)
    inv_sq = 1.0 / norm_sq
    alpha1 = (m00 + m01) * inv_sq
    c = 1.0 - alpha1
    res_sq = (m11 + c * (2.0 * m01 + c * m00)) * inv_sq
    beta1 = jnp.sqrt(jnp.maximum(res_sq, 0.0) + epsilon)
    k2 = 1.0 / (start_norm * beta1)
    n11 = m11 + c * (2.0 * m01 + c * m00)
    n12 = m12 + c * (2.0 * m11 + c * m01)
    alpha2 = k2 * k2 * (n11 + n12)
    f1 = 1.0 + c - alpha2
    f0 = c - alpha2 * c - beta1 * beta1
    n22 = m22 + f1 * (2.0 * m12 + f1 * m11) + f0 * (2.0 * (m11 + f1 * m01) + f0 * m00)
    beta2 = jnp.sqrt(jnp.maximum(k2 * k2 * n22, 0.0) + epsilon)
    k3 = k2 / beta2
    n23 = m23 + f1 * (2.0 * m22 + f1 * m12) + f0 * (2.0 * (m12 + f1 * m11) + f0 * m01)
    alpha3 = k3 * k3 * (jnp.maximum(n22, 0.0) + n23)

    scale = (alpha1 + alpha2 + alpha3) / 3.0
    inv_scale = 1.0 / scale
    zero, one = jnp.zeros_like(scale), jnp.ones_like(scale)
    y = (alpha1 * inv_scale, beta1 * inv_scale, zero, alpha2 * inv_scale, beta2 * inv_scale, alpha3 * inv_scale)
    z = (one, zero, zero, one, zero, one)
    for _ in range(ROOT_ITERS):
        inv_z, inv_y = inverse_symmetric(z), inverse_symmetric(y)
        y = tuple(0.5 * (p + q) for p, q in zip(y, inv_z))
        z = tuple(0.5 * (p + q) for p, q in zip(z, inv_y))
    root_scale = jnp.sqrt(scale)
    r1, r2, r3 = root_scale * y[0], root_scale * y[1], root_scale * y[2]
    w2, w3 = start_norm * r2 * k2, start_norm * r3 * k3
    p0 = r1 + w2 * c + w3 * f0
    p1 = w2 + w3 * f1
    for block in range(blocks):
        for c in range(3):
            at = pl.ds(c * samples, samples)
            out = p0 * x0_ref[block, at] + p1 * x1_ref[block, at] + w3 * x2_ref[block, at]
            out_ref[0, 0, block, :, pl.ds(c * beads, beads)] = out


def call(kernel, outs, in_specs, scratch=(), limit=None, cost=None):
    return pl.pallas_call(
        kernel,
        out_shape=outs,
        in_specs=in_specs,
        out_specs=jax.tree.map(lambda _: VMEM, outs),
        scratch_shapes=list(scratch),
        compiler_params=pltpu.CompilerParams(vmem_limit_bytes=limit),
        cost_estimate=cost,
    )


def body(positions, block_fill, noise, pair_list, pair_count):
    blocks, beads = positions.shape[2], positions.shape[4]
    samples = noise.shape[3]
    rows = 3 * samples
    shape = (blocks, rows, beads)
    devices = lax.axis_size(AXES)
    columns_x = 2 if lax.axis_size("gx") == 2 else 3
    columns = columns_x * (2 if lax.axis_size("gy") == 2 else 3)
    sides = 1 if lax.axis_size("gz") == 2 else 2
    near_slots, far_slots = columns * blocks, columns * sides
    limit = 8 << 20

    x0, mask, packed = call(
        pack_kernel,
        (
            jax.ShapeDtypeStruct(shape, f32),
            jax.ShapeDtypeStruct((blocks, 8, beads), f32),
            jax.ShapeDtypeStruct((blocks, rows + 16, beads), bf16),
        ),
        [HBM] * 3,
        (
            pltpu.SMEM(block_fill.shape, jnp.int32),
            pltpu.VMEM(noise.shape, f32),
            pltpu.VMEM((1, 1, 3, blocks, beads), f32),
            pltpu.SemaphoreType.DMA((3,)),
        ),
        4 << 20,
    )(*[pltpu.with_memory_space_constraint(a, pltpu.HBM) for a in (block_fill, noise, jnp.swapaxes(positions, 2, 3))])
    near_table, far_table = pair_tables(pair_list, pair_count, blocks, near_slots, far_slots)
    field, sent = jax.ShapeDtypeStruct(shape, f32), jax.ShapeDtypeStruct(shape, bf16)
    tile = jax.ShapeDtypeStruct((pair_list.shape[4] // GROUP + blocks, 2 * beads, len(PLACES) * beads), bf16)
    total = pltpu.VMEM(shape, f32)
    turned = (pltpu.VMEM((beads, 128), f32),) * 2
    cost = pl.CostEstimate(flops=10**8, bytes_accessed=10**7, transcendentals=0)

    def slots(count, rows):
        return pltpu.VMEM((count + 1, rows, beads), bf16)

    part, far, near_table, far_table = spread(packed, near_table, far_table)
    even_n, odd_n, near = call(
        build_near,
        (tile, tile, field),
        [SMEM] + [VMEM] * 2,
        (slots(near_slots, rows + 16),) + turned,
        limit,
        cost,
    )(near_table, packed, part)
    even_f, odd_f, x1, send = call(
        functools.partial(build_far, sides),
        (tile, tile, field, sent),
        [SMEM] + [VMEM] * (4 + sides),
        (slots(far_slots, rows + 16), total) + turned,
        limit,
    )(far_table, packed, mask, x0, near, *far)

    def near_product(part):
        return call(
            apply_near, field, [SMEM] + [VMEM] * 3, (slots(near_slots, rows),), limit, cost
        )(near_table, even_n, odd_n, part)

    part, far = spread(send)
    near = near_product(part)
    x2, send = call(
        functools.partial(apply_far, sides),
        (field, sent),
        [SMEM] + [VMEM] * (5 + sides),
        (slots(far_slots, rows), total),
        limit,
    )(far_table, even_f, odd_f, mask, x1, near, *far)
    part, far = spread(send)
    near = near_product(part)
    moments = call(
        functools.partial(last_far, sides),
        jax.ShapeDtypeStruct((devices, 1, 128), f32),
        [SMEM] + [VMEM] * (7 + sides),
        (slots(far_slots, rows), total),
        limit,
    )(far_table, even_f, odd_f, mask, x0, x1, x2, near, *far)
    moments = lax.all_to_all(moments, AXES, 0, 0)
    return call(final_kernel, jax.ShapeDtypeStruct(noise.shape, f32), [VMEM] * 4, (), 4 << 20)(moments, x0, x1, x2)


def solution(mesh):
    block = P("gx", "gy", "gz", None, None)
    cell = P("gx", "gy", "gz")
    return jax.shard_map(
        body, mesh=mesh, in_specs=(block, cell, block, block, cell), out_specs=block, check_vma=False
    )
```

```python
import functools

import jax
import jax.numpy as jnp
from jax import lax
from jax.experimental import pallas as pl
from jax.experimental.pallas import tpu as pltpu
from jax.sharding import PartitionSpec as P

ITERS = 3
ROOT_ITERS = 12
CHUNK = 16

radius = 0.08
floor_sq = 0.0001
epsilon = 1e-06

AXES = ("gx", "gy", "gz")
VMEM = pl.BlockSpec(memory_space=pltpu.VMEM)
HBM = pl.BlockSpec(memory_space=pltpu.HBM)
SMEM = pl.BlockSpec(memory_space=pltpu.SMEM)
f32 = jnp.float32
bf16 = jnp.bfloat16
PLACES = ((0, 0), (0, 1), (0, 2), (1, 1), (1, 2), (2, 2))


def matching(count, parity):
    pairs = []
    for i in range(parity, count - 1, 2):
        pairs += [(i, i + 1), (i + 1, i)]
    return pairs


def swaps(axis, first, second):
    count = lax.axis_size(axis)
    got = [lax.ppermute(first, axis, matching(count, 0))]
    if count > 2:
        got.append(lax.ppermute(second, axis, matching(count, 1)))
    return got


def spread(field, table, stage):
    shape = (-1,) + field.shape[1:]
    columns = jnp.stack([field] + swaps("gx", field, field))
    columns, table = lax.optimization_barrier((columns, table))
    others = swaps("gy", columns, columns)
    result = stage(table, 0, [columns.reshape(shape)], None)
    odd = lax.axis_index("gz") % 2 == 1
    low = jnp.concatenate([part[:, 0] for part in [columns] + others])
    high = jnp.concatenate([part[:, field.shape[0] - 1] for part in [columns] + others])
    low, high, result = lax.optimization_barrier((jnp.where(odd, low, high), jnp.where(odd, high, low), result))
    far = swaps("gz", low, high)
    result = stage(table, 1, [part.reshape(shape) for part in others], result)
    return stage(table, 2, far, result)


def table_kernel(sizes, slots, blocks, count_ref, list_hbm, table_ref, list_ref, sem):
    copy = pltpu.make_async_copy(list_hbm, list_ref, sem)
    copy.start()
    sets = len(slots) * blocks
    segment = table_ref.shape[1] // sets
    for i in range(sets):
        table_ref[1, i] = 0
    odd = [lax.rem(lax.axis_index(axis), 2) == 1 for axis in AXES]

    def partner(axis, step):
        if sizes[axis] == 2:
            return jnp.where(step == 0, 0, 1)
        return jnp.where(step == 0, 0, jnp.where((step < 0) == odd[axis], 1, 2))

    def enter(t, carry):
        home, code = list_ref[0, 0, 0, 0, t], list_ref[0, 0, 1, 0, t]
        plane, third = (code * 57) >> 9, (code * 43) >> 7
        x, y = partner(0, plane - 1), partner(1, third - 3 * plane - 1)
        z = home + code - 3 * third - 1
        far = (z < 0) | (z >= blocks)
        width = slots[0] // blocks
        side = partner(2, jnp.where(z < 0, -1, 1)) - 1
        slot = (jnp.maximum(y - 1, 0) * width + x) * blocks + z
        slot = jnp.where(far, side * (slots[2] // (1 if sizes[2] == 2 else 2)) + y * width + x, slot)
        at = jnp.where(far, 2, jnp.minimum(y, 1)) * blocks + home
        place = table_ref[1, at]
        table_ref[1, at] = place + 1
        table_ref[0, at * segment + place] = slot
        return carry

    copy.wait()
    lax.fori_loop(0, count_ref[0, 0, 0], enter, 0)
    for stage, empty in enumerate(slots):
        for block in range(blocks):
            at = stage * blocks + block
            end = at * segment + table_ref[1, at]
            for i in range(3):
                table_ref[0, end + i] = empty


def pair_table(pair_list, pair_count, blocks, slots):
    segment = -(-(pair_list.shape[4] + 3) // 2) * 2
    sizes = [lax.axis_size(axis) for axis in AXES]
    pair_list = pltpu.with_memory_space_constraint(jnp.swapaxes(pair_list, 2, 3), pltpu.HBM)
    return pl.pallas_call(
        functools.partial(table_kernel, sizes, slots, blocks),
        out_shape=jax.ShapeDtypeStruct((2, len(slots) * blocks * segment), jnp.int32),
        in_specs=[SMEM, HBM],
        out_specs=SMEM,
        scratch_shapes=[pltpu.SMEM(pair_list.shape, jnp.int32), pltpu.SemaphoreType.DMA],
        compiler_params=pltpu.CompilerParams(vmem_limit_bytes=1 << 20),
        cost_estimate=pl.CostEstimate(flops=10**6, bytes_accessed=10**6, transcendentals=0),
    )(pair_count, pair_list)


def duos_of(table_ref, stage, blocks):
    segment = table_ref.shape[1] // (3 * blocks)
    counts = [(table_ref[1, stage * blocks + block] + 1) >> 1 for block in range(blocks)]
    ends = [sum(counts[: block + 1]) for block in range(blocks)]

    def home_of(duo):
        return sum([jnp.where(duo >= end, 1, 0) for end in ends[:-1]], 0)

    def first_of(duo):
        skip = [jnp.where(duo >= ends[i], segment - 2 * counts[i], 0) for i in range(blocks - 1)]
        return stage * blocks * segment + 2 * duo + sum(skip)

    return ends[-1], home_of, first_of


def pack_kernel(fill_hbm, noise_hbm, pos_hbm, start_ref, mask_ref, pack_ref, fill_ref, noise_ref, pos_ref, sems):
    pairs = ((fill_hbm, fill_ref), (noise_hbm, noise_ref), (pos_hbm, pos_ref))
    copies = [pltpu.make_async_copy(a, b, sems.at[i]) for i, (a, b) in enumerate(pairs)]
    for copy in copies:
        copy.start()
    for copy in copies:
        copy.wait()
    blocks, samples, width = noise_ref.shape[2:]
    beads = width // 3
    row = lax.broadcasted_iota(jnp.int32, (16, beads), 0)
    for block in range(blocks):
        mask = (lax.broadcasted_iota(jnp.int32, (8, beads), 1) < fill_ref[0, 0, block]).astype(f32)
        mask_ref[block] = mask
        noise = [noise_ref[0, 0, block, :, pl.ds(c * beads, beads)] for c in range(3)]
        start = jnp.concatenate([part * mask[:1] for part in noise], axis=0)
        start_ref[block] = start
        place = jnp.zeros((16, beads), f32)
        for c in range(3):
            pos = pos_ref[0, 0, c, pl.ds(block, 1)]
            high = pos.astype(bf16).astype(f32)
            rest = pos - high
            mid = rest.astype(bf16).astype(f32)
            for i, piece in ((0, high), (8, mid), (3, rest - mid)):
                place = jnp.where(row == i + c, piece, place)
        pack_ref[block] = jnp.concatenate([start, place], axis=0).astype(bf16)


def gather_slots(parts, slots_ref):
    count = parts[0].shape[0]
    for i, part in enumerate(parts):
        slots_ref[pl.ds(i * count, count)] = part[...]
    slots_ref[len(parts) * count] = jnp.zeros(slots_ref.shape[1:], bf16)


def position_of(slots_ref, slot, field_rows):
    rows = slots_ref[slot].astype(f32)[field_rows:]
    return rows[:8] + rows[8:] + pltpu.roll(rows[:8], 5, 0)


def turn_positions(slots_ref, first, second, field_rows):
    first = position_of(slots_ref, first, field_rows)
    second = pltpu.roll(position_of(slots_ref, second, field_rows), 3, 0)
    row = lax.broadcasted_iota(jnp.int32, first.shape, 0)
    return jnp.transpose(jnp.where(row < 3, first, second))


def make_tile(home, turned_ref, tiles_ref, pair, half):
    beads = home.shape[1]
    base = half * beads
    for first in range(0, beads, CHUNK):
        turned = turned_ref[pl.ds(first, CHUNK)]
        d = [turned[:, 3 * half + c : 3 * half + c + 1] - home[c : c + 1] for c in range(3)]
        dist_sq = d[0] * d[0] + d[1] * d[1] + d[2] * d[2]
        root = lax.rsqrt(jnp.maximum(dist_sq, 1e-30))
        distance = dist_sq * root
        inv_root = jnp.minimum(root, floor_sq**-0.5)
        inverse_sq = inv_root * inv_root
        far = (0.75 * radius) * inv_root
        far_two = (2.0 * radius * radius) * (far * inverse_sq)
        apart = dist_sq >= 4.0 * radius * radius
        isotropic = jnp.where(apart, far + far_two * (1.0 / 3.0), 1.0 - (9.0 / 32.0 / radius) * distance)
        dyadic = jnp.where(apart, far - far_two, (3.0 / 32.0 / radius) * distance) * inverse_sq
        scaled = [dyadic * d[c] for c in range(3)]
        entries = []
        for c, e in PLACES:
            entry = scaled[c] * d[e]
            entries.append(entry + isotropic if c == e else entry)
        tiles_ref[pair, pl.ds(base + first, CHUNK)] = jnp.concatenate(entries, axis=1).astype(bf16)


def add_product(sum_ref, home, product):
    rows, beads = sum_ref.shape[1:]
    samples = rows // 3
    out = [0.0] * 3
    for k, (c, e) in enumerate(PLACES):
        column = product[:, k * beads : (k + 1) * beads]
        out[c] = out[c] + column[e * samples : (e + 1) * samples]
        if c != e:
            out[e] = out[e] + column[c * samples : (c + 1) * samples]
    sum_ref[home] = sum_ref[home] + jnp.concatenate(out, axis=0)


def field_of(table_ref, slots_ref, first, rows):
    return jnp.concatenate([slots_ref[table_ref[0, first + i]][:rows] for i in range(2)], axis=1)


def product(field, tile):
    return jnp.dot(field, tile, preferred_element_type=f32)


def multiply(table_ref, stage, slots_ref, even_ref, odd_ref, sum_ref):
    blocks, rows = sum_ref.shape[:2]
    count, home_of, first_of = duos_of(table_ref, stage, blocks)

    def both(turn, carry):
        duo = 2 * turn
        odd = jnp.where(duo + 1 < count, turn, 0)
        first = product(field_of(table_ref, slots_ref, first_of(duo), rows), even_ref[turn])
        second = product(field_of(table_ref, slots_ref, first_of(duo + 1), rows), odd_ref[odd])
        add_product(sum_ref, home_of(duo), first)
        add_product(sum_ref, jnp.minimum(home_of(duo + 1), blocks - 1), second)
        return carry

    lax.fori_loop(0, (count + 1) >> 1, both, 0)


def build(table_ref, stage, own_ref, slots_ref, even_ref, odd_ref, sum_ref, turn_even, turn_odd):
    blocks, rows = sum_ref.shape[:2]
    count, home_of, first_of = duos_of(table_ref, stage, blocks)
    odd_ref[0] = jnp.zeros(odd_ref.shape[1:], bf16)

    def prepare(duo, columns_ref):
        first = first_of(duo)
        columns_ref[:, :8] = turn_positions(slots_ref, table_ref[0, first], table_ref[0, first + 1], rows)

    def consume(duo, tile, index):
        field = field_of(table_ref, slots_ref, first_of(duo), rows)
        add_product(sum_ref, jnp.minimum(home_of(duo), blocks - 1), product(field, tile[index]))

    def make(duo, columns_ref, tile, index):
        place = position_of(own_ref, home_of(duo), rows)
        for i in range(2):
            make_tile(place, columns_ref, tile, index, i)

    def both(turn, spare):
        duo = 2 * turn
        full = duo + 1 < count
        make(duo, turn_even, even_ref, turn)
        prepare(duo + 1, turn_odd)
        consume(jnp.where(turn == 0, count, duo - 1), odd_ref, spare)

        @pl.when(full)
        def _():
            make(duo + 1, turn_odd, odd_ref, turn)
            prepare(duo + 2, turn_even)
            consume(duo, even_ref, turn)

        @pl.when(jnp.logical_not(full))
        def _():
            consume(duo, even_ref, turn)

        return jnp.where(full, turn, spare)

    prepare(0, turn_even)
    spare = lax.fori_loop(0, (count + 1) >> 1, both, 0)
    consume(jnp.where(count % 2 == 0, jnp.maximum(count - 1, 0), count), odd_ref, spare)


def new_field(block, mask_ref, sum_ref, old_ref):
    return sum_ref[block] * mask_ref[block, :1] - old_ref[block]


def stage_kernel(stage, building, moments, *refs):
    refs = list(refs)
    table_ref, own_ref = refs.pop(0), refs.pop(0) if building else None
    tiles = None if building else (refs.pop(0), refs.pop(0))
    before_ref = refs.pop(0) if stage else None
    last = stage == 2
    mask_ref = refs.pop(0) if last else None
    old = [refs.pop(0) for _ in range(3 if moments else 1)] if last else []
    columns = [refs.pop(), refs.pop()] if building else []
    sum_ref = refs.pop() if last else None
    slots_ref = refs.pop()
    outs = [refs.pop() for _ in range(1 if moments or not last else 2)][::-1]
    if building:
        tiles = [refs.pop(), refs.pop()][::-1]
    gather_slots(refs, slots_ref)
    if not last:
        sum_ref = outs[0]
    sum_ref[...] = before_ref[...] if stage else jnp.zeros_like(sum_ref)
    if building:
        build(table_ref, stage, own_ref, slots_ref, *tiles, sum_ref, *columns)
    else:
        multiply(table_ref, stage, slots_ref, *tiles, sum_ref)
    if moments:
        take_moments(mask_ref, sum_ref, *old, outs[0])
    elif last:
        for block in range(sum_ref.shape[0]):
            new = new_field(block, mask_ref, sum_ref, old[0])
            outs[0][block] = new
            outs[1][block] = new.astype(bf16)


MOMENTS = ((0, 0), (0, 1), (1, 1), (1, 2), (2, 2), (2, 3))


def take_moments(mask_ref, sum_ref, x0_ref, x1_ref, x2_ref, moment_ref):
    blocks, rows, beads = x0_ref.shape
    samples = rows // 3
    lanes = moment_ref.shape[2]
    lane = lax.broadcasted_iota(jnp.int32, (samples, lanes), 1)
    row = lax.broadcasted_iota(jnp.int32, (samples, lanes), 0)
    sums = [0.0] * len(MOMENTS)
    for block in range(blocks):
        x = [x0_ref[block], x1_ref[block], x2_ref[block]]
        x.append(new_field(block, mask_ref, sum_ref, x2_ref))
        for k, (i, j) in enumerate(MOMENTS):
            both = x[i] * x[j]
            sums[k] = sums[k] + both[:samples] + both[samples : 2 * samples] + both[2 * samples :]
    grid = jnp.zeros((samples, lanes), f32)
    for k, value in enumerate(sums):
        value = jnp.sum(value, axis=1, keepdims=True)
        grid = jnp.where(lane == row + k * samples, value, grid)
    line = jnp.sum(grid, axis=0, keepdims=True)
    moment_ref[...] = jnp.broadcast_to(line[None], moment_ref.shape)


def inverse_symmetric(m):
    a, b, c, d, e, f = m
    ca, cb, cc = d * f - e * e, c * e - b * f, b * e - c * d
    scale = 1.0 / (a * ca + b * cb + c * cc)
    return (ca * scale, cb * scale, cc * scale, (a * f - c * c) * scale, (b * c - a * e) * scale, (a * d - b * b) * scale)


def final_kernel(moment_ref, x0_ref, x1_ref, x2_ref, out_ref):
    blocks, rows, beads = x0_ref.shape
    samples = rows // 3
    lanes = moment_ref.shape[2]
    lane = lax.broadcasted_iota(jnp.int32, (samples, lanes), 1)
    row = lax.broadcasted_iota(jnp.int32, (samples, lanes), 0)
    line = jnp.broadcast_to(jnp.sum(moment_ref[...], axis=0), (samples, lanes))
    m00, m01, m11, m12, m22, m23 = [
        jnp.broadcast_to(
            jnp.sum(jnp.where(lane == row + k * samples, line, 0.0), axis=1, keepdims=True), (samples, lanes)
        )
        for k in range(len(MOMENTS))
    ]
    norm_sq = m00 + epsilon
    start_norm = jnp.sqrt(norm_sq)
    inv_sq = 1.0 / norm_sq
    alpha1 = (m00 + m01) * inv_sq
    c = 1.0 - alpha1
    res_sq = (m11 + c * (2.0 * m01 + c * m00)) * inv_sq
    beta1 = jnp.sqrt(jnp.maximum(res_sq, 0.0) + epsilon)
    k2 = 1.0 / (start_norm * beta1)
    n11 = m11 + c * (2.0 * m01 + c * m00)
    n12 = m12 + c * (2.0 * m11 + c * m01)
    alpha2 = k2 * k2 * (n11 + n12)
    f1 = 1.0 + c - alpha2
    f0 = c - alpha2 * c - beta1 * beta1
    n22 = m22 + f1 * (2.0 * m12 + f1 * m11) + f0 * (2.0 * (m11 + f1 * m01) + f0 * m00)
    beta2 = jnp.sqrt(jnp.maximum(k2 * k2 * n22, 0.0) + epsilon)
    k3 = k2 / beta2
    n23 = m23 + f1 * (2.0 * m22 + f1 * m12) + f0 * (2.0 * (m12 + f1 * m11) + f0 * m01)
    alpha3 = k3 * k3 * (jnp.maximum(n22, 0.0) + n23)

    scale = (alpha1 + alpha2 + alpha3) / 3.0
    inv_scale = 1.0 / scale
    zero, one = jnp.zeros_like(scale), jnp.ones_like(scale)
    y = (alpha1 * inv_scale, beta1 * inv_scale, zero, alpha2 * inv_scale, beta2 * inv_scale, alpha3 * inv_scale)
    z = (one, zero, zero, one, zero, one)
    for _ in range(ROOT_ITERS):
        inv_z, inv_y = inverse_symmetric(z), inverse_symmetric(y)
        y = tuple(0.5 * (p + q) for p, q in zip(y, inv_z))
        z = tuple(0.5 * (p + q) for p, q in zip(z, inv_y))
    root_scale = jnp.sqrt(scale)
    r1, r2, r3 = root_scale * y[0], root_scale * y[1], root_scale * y[2]
    w2, w3 = start_norm * r2 * k2, start_norm * r3 * k3
    p0 = r1 + w2 * c + w3 * f0
    p1 = w2 + w3 * f1
    for block in range(blocks):
        for c in range(3):
            at = pl.ds(c * samples, samples)
            out = p0 * x0_ref[block, at] + p1 * x1_ref[block, at] + w3 * x2_ref[block, at]
            out_ref[0, 0, block, :, pl.ds(c * beads, beads)] = out


def call(kernel, outs, in_specs, scratch=(), limit=None, cost=None):
    return pl.pallas_call(
        kernel,
        out_shape=outs,
        in_specs=in_specs,
        out_specs=jax.tree.map(lambda _: VMEM, outs),
        scratch_shapes=list(scratch),
        compiler_params=pltpu.CompilerParams(vmem_limit_bytes=limit),
        cost_estimate=cost,
    )


def body(positions, block_fill, noise, pair_list, pair_count):
    blocks, beads = positions.shape[2], positions.shape[4]
    samples = noise.shape[3]
    rows = 3 * samples
    shape = (blocks, rows, beads)
    devices = lax.axis_size(AXES)
    columns = 2 if lax.axis_size("gx") == 2 else 3
    others = 1 if lax.axis_size("gy") == 2 else 2
    sides = 1 if lax.axis_size("gz") == 2 else 2
    slots = (columns * blocks, others * columns * blocks, sides * (1 + others) * columns)
    limit = 8 << 20

    x0, mask, packed = call(
        pack_kernel,
        (
            jax.ShapeDtypeStruct(shape, f32),
            jax.ShapeDtypeStruct((blocks, 8, beads), f32),
            jax.ShapeDtypeStruct((blocks, rows + 16, beads), bf16),
        ),
        [HBM] * 3,
        (
            pltpu.SMEM(block_fill.shape, jnp.int32),
            pltpu.VMEM(noise.shape, f32),
            pltpu.VMEM((1, 1, 3, blocks, beads), f32),
            pltpu.SemaphoreType.DMA((3,)),
        ),
        4 << 20,
    )(*[pltpu.with_memory_space_constraint(a, pltpu.HBM) for a in (block_fill, noise, jnp.swapaxes(positions, 2, 3))])
    table = pair_table(pair_list, pair_count, blocks, slots)
    field, sent = jax.ShapeDtypeStruct(shape, f32), jax.ShapeDtypeStruct(shape, bf16)
    capacity = (pair_list.shape[4] + blocks) // 4 + 1
    tile = jax.ShapeDtypeStruct((capacity, 2 * beads, len(PLACES) * beads), bf16)
    total = pltpu.VMEM(shape, f32)
    moment = jax.ShapeDtypeStruct((devices, 1, 128), f32)
    cost = pl.CostEstimate(flops=10**8, bytes_accessed=10**7, transcendentals=0)

    def apply(vector, tiles, olds):
        building, moments = not tiles, len(olds) == 3

        def stage(table, index, given, result):
            last = index == 2
            outs = (moment,) if last and moments else (field, sent) if last else (field,)
            scratch = [pltpu.VMEM((slots[index] + 1,) + given[0].shape[1:], bf16)]
            scratch += [total] * last + [pltpu.VMEM((beads, 128), f32)] * (2 * building)
            args = [packed] if building else list(tiles[index])
            args += ([result] if index else []) + ([mask] + olds if last else []) + given
            result = call(
                functools.partial(stage_kernel, index, building, last and moments),
                (tile, tile) * building + outs,
                [SMEM] + [VMEM] * len(args),
                scratch,
                limit,
                None if last else cost,
            )(table, *args)
            if building:
                tiles.append(result[:2])
                result = result[2:]
            return result if last and not moments else result[0]

        return spread(vector, table, stage)

    tiles = []
    x1, send = apply(packed, tiles, [x0])
    x2, send = apply(send, tiles, [x1])
    moments = apply(send, tiles, [x0, x1, x2])
    moments = lax.all_to_all(moments, AXES, 0, 0)
    return call(final_kernel, jax.ShapeDtypeStruct(noise.shape, f32), [VMEM] * 4, (), 4 << 20)(moments, x0, x1, x2)


def solution(mesh):
    block = P("gx", "gy", "gz", None, None)
    cell = P("gx", "gy", "gz")
    return jax.shard_map(
        body, mesh=mesh, in_specs=(block, cell, block, block, cell), out_specs=block, check_vma=False
    )
```

```python
import functools

import jax
import jax.numpy as jnp
from jax import lax
from jax.experimental import pallas as pl
from jax.experimental.pallas import tpu as pltpu
from jax.sharding import PartitionSpec as P

ITERS = 3
ROOT_ITERS = 12
CHUNK = 16

radius = 0.08
floor_sq = 0.0001
epsilon = 1e-06

AXES = ("gx", "gy", "gz")
VMEM = pl.BlockSpec(memory_space=pltpu.VMEM)
HBM = pl.BlockSpec(memory_space=pltpu.HBM)
SMEM = pl.BlockSpec(memory_space=pltpu.SMEM)
f32 = jnp.float32
bf16 = jnp.bfloat16
PLACES = ((0, 0), (0, 1), (0, 2), (1, 1), (1, 2), (2, 2))


def matching(count, parity):
    pairs = []
    for i in range(parity, count - 1, 2):
        pairs += [(i, i + 1), (i + 1, i)]
    return pairs


def swaps(axis, first, second):
    count = lax.axis_size(axis)
    got = [lax.ppermute(first, axis, matching(count, 0))]
    if count > 2:
        got.append(lax.ppermute(second, axis, matching(count, 1)))
    return got


def plane_exchange(field):
    plane = ("gx", "gy")
    size_x, size_y = [lax.axis_size(axis) for axis in plane]
    got = lax.all_to_all(jnp.broadcast_to(field[None], (size_x * size_y,) + field.shape), plane, 0, 0)
    x, y = [lax.axis_index(axis) for axis in plane]

    def partners(index, count):
        even, odd = index + 1 - 2 * (index % 2), index - 1 + 2 * (index % 2)
        return [index, jnp.minimum(even, count - 1)] + [jnp.clip(odd, 0, count - 1)] * (count > 2)

    rows = [
        jnp.stack([lax.dynamic_index_in_dim(got, i * size_y + j, 0, False) for i in partners(x, size_x)])
        for j in partners(y, size_y)
    ]
    return rows[0], rows[1:]


def spread(field, table, stage, at_once):
    shape = (-1,) + field.shape[1:]
    if at_once:
        columns, others = plane_exchange(field)
    else:
        columns = jnp.stack([field] + swaps("gx", field, field))
        columns, table = lax.optimization_barrier((columns, table))
        others = swaps("gy", columns, columns)
    result = stage(table, 0, [columns.reshape(shape)], None)
    odd = lax.axis_index("gz") % 2 == 1
    low = jnp.concatenate([part[:, 0] for part in [columns] + others])
    high = jnp.concatenate([part[:, field.shape[0] - 1] for part in [columns] + others])
    low, high = jnp.where(odd, low, high), jnp.where(odd, high, low)
    if not at_once:
        low, high, result = lax.optimization_barrier((low, high, result))
    far = swaps("gz", low, high)
    result = stage(table, 1, [part.reshape(shape) for part in others], result)
    return stage(table, 2, far, result)


def table_kernel(sizes, slots, blocks, count_ref, list_hbm, table_ref, list_ref, sem):
    copy = pltpu.make_async_copy(list_hbm, list_ref, sem)
    copy.start()
    sets = len(slots) * blocks
    segment = table_ref.shape[1] // sets
    for i in range(sets):
        table_ref[1, i] = 0
    odd = [lax.rem(lax.axis_index(axis), 2) == 1 for axis in AXES]

    def partner(axis, step):
        if sizes[axis] == 2:
            return jnp.where(step == 0, 0, 1)
        return jnp.where(step == 0, 0, jnp.where((step < 0) == odd[axis], 1, 2))

    def enter(t, carry):
        home, code = list_ref[0, 0, 0, 0, t], list_ref[0, 0, 1, 0, t]
        plane, third = (code * 57) >> 9, (code * 43) >> 7
        x, y = partner(0, plane - 1), partner(1, third - 3 * plane - 1)
        z = home + code - 3 * third - 1
        far = (z < 0) | (z >= blocks)
        width = slots[0] // blocks
        side = partner(2, jnp.where(z < 0, -1, 1)) - 1
        slot = (jnp.maximum(y - 1, 0) * width + x) * blocks + z
        slot = jnp.where(far, side * (slots[2] // (1 if sizes[2] == 2 else 2)) + y * width + x, slot)
        at = jnp.where(far, 2, jnp.minimum(y, 1)) * blocks + home
        place = table_ref[1, at]
        table_ref[1, at] = place + 1
        table_ref[0, at * segment + place] = slot
        return carry

    copy.wait()
    lax.fori_loop(0, count_ref[0, 0, 0], enter, 0)
    for stage, empty in enumerate(slots):
        for block in range(blocks):
            at = stage * blocks + block
            end = at * segment + table_ref[1, at]
            for i in range(3):
                table_ref[0, end + i] = empty


def pair_table(pair_list, pair_count, blocks, slots):
    segment = -(-(pair_list.shape[4] + 3) // 2) * 2
    sizes = [lax.axis_size(axis) for axis in AXES]
    pair_list = pltpu.with_memory_space_constraint(jnp.swapaxes(pair_list, 2, 3), pltpu.HBM)
    return pl.pallas_call(
        functools.partial(table_kernel, sizes, slots, blocks),
        out_shape=jax.ShapeDtypeStruct((2, len(slots) * blocks * segment), jnp.int32),
        in_specs=[SMEM, HBM],
        out_specs=SMEM,
        scratch_shapes=[pltpu.SMEM(pair_list.shape, jnp.int32), pltpu.SemaphoreType.DMA],
        compiler_params=pltpu.CompilerParams(vmem_limit_bytes=1 << 20),
        cost_estimate=pl.CostEstimate(flops=10**6, bytes_accessed=10**6, transcendentals=0),
    )(pair_count, pair_list)


def duos_of(table_ref, stage, blocks):
    segment = table_ref.shape[1] // (3 * blocks)
    counts = [(table_ref[1, stage * blocks + block] + 1) >> 1 for block in range(blocks)]
    ends = [sum(counts[: block + 1]) for block in range(blocks)]

    def home_of(duo):
        return sum([jnp.where(duo >= end, 1, 0) for end in ends[:-1]], 0)

    def first_of(duo):
        skip = [jnp.where(duo >= ends[i], segment - 2 * counts[i], 0) for i in range(blocks - 1)]
        return stage * blocks * segment + 2 * duo + sum(skip)

    return ends[-1], home_of, first_of


def pack_kernel(fill_hbm, noise_hbm, pos_hbm, start_ref, mask_ref, pack_ref, fill_ref, noise_ref, pos_ref, sems):
    pairs = ((fill_hbm, fill_ref), (noise_hbm, noise_ref), (pos_hbm, pos_ref))
    copies = [pltpu.make_async_copy(a, b, sems.at[i]) for i, (a, b) in enumerate(pairs)]
    for copy in copies:
        copy.start()
    for copy in copies:
        copy.wait()
    blocks, samples, width = noise_ref.shape[2:]
    beads = width // 3
    row = lax.broadcasted_iota(jnp.int32, (16, beads), 0)
    for block in range(blocks):
        mask = (lax.broadcasted_iota(jnp.int32, (8, beads), 1) < fill_ref[0, 0, block]).astype(f32)
        mask_ref[block] = mask
        noise = [noise_ref[0, 0, block, :, pl.ds(c * beads, beads)] for c in range(3)]
        start = jnp.concatenate([part * mask[:1] for part in noise], axis=0)
        start_ref[block] = start
        place = jnp.zeros((16, beads), f32)
        for c in range(3):
            pos = pos_ref[0, 0, c, pl.ds(block, 1)]
            high = pos.astype(bf16).astype(f32)
            rest = pos - high
            mid = rest.astype(bf16).astype(f32)
            for i, piece in ((0, high), (8, mid), (3, rest - mid)):
                place = jnp.where(row == i + c, piece, place)
        pack_ref[block] = jnp.concatenate([start, place], axis=0).astype(bf16)


def gather_slots(parts, slots_ref):
    count = parts[0].shape[0]
    for i, part in enumerate(parts):
        slots_ref[pl.ds(i * count, count)] = part[...]
    slots_ref[len(parts) * count] = jnp.zeros(slots_ref.shape[1:], bf16)


def position_of(slots_ref, slot, field_rows):
    rows = slots_ref[slot].astype(f32)[field_rows:]
    return rows[:8] + rows[8:] + pltpu.roll(rows[:8], 5, 0)


def turn_positions(slots_ref, first, second, field_rows):
    first = position_of(slots_ref, first, field_rows)
    second = pltpu.roll(position_of(slots_ref, second, field_rows), 3, 0)
    row = lax.broadcasted_iota(jnp.int32, first.shape, 0)
    return jnp.transpose(jnp.where(row < 3, first, second))


def make_tile(home, turned_ref, tiles_ref, pair, half):
    beads = home.shape[1]
    base = half * beads
    for first in range(0, beads, CHUNK):
        turned = turned_ref[pl.ds(first, CHUNK)]
        d = [turned[:, 3 * half + c : 3 * half + c + 1] - home[c : c + 1] for c in range(3)]
        dist_sq = d[0] * d[0] + d[1] * d[1] + d[2] * d[2]
        root = lax.rsqrt(jnp.maximum(dist_sq, 1e-30))
        distance = dist_sq * root
        inv_root = jnp.minimum(root, floor_sq**-0.5)
        inverse_sq = inv_root * inv_root
        far = (0.75 * radius) * inv_root
        far_two = (2.0 * radius * radius) * (far * inverse_sq)
        apart = dist_sq >= 4.0 * radius * radius
        isotropic = jnp.where(apart, far + far_two * (1.0 / 3.0), 1.0 - (9.0 / 32.0 / radius) * distance)
        dyadic = jnp.where(apart, far - far_two, (3.0 / 32.0 / radius) * distance) * inverse_sq
        scaled = [dyadic * d[c] for c in range(3)]
        entries = []
        for c, e in PLACES:
            entry = scaled[c] * d[e]
            entries.append(entry + isotropic if c == e else entry)
        tiles_ref[pair, pl.ds(base + first, CHUNK)] = jnp.concatenate(entries, axis=1).astype(bf16)


def add_product(sum_ref, home, product):
    rows, beads = sum_ref.shape[1:]
    samples = rows // 3
    out = [0.0] * 3
    for k, (c, e) in enumerate(PLACES):
        column = product[:, k * beads : (k + 1) * beads]
        out[c] = out[c] + column[e * samples : (e + 1) * samples]
        if c != e:
            out[e] = out[e] + column[c * samples : (c + 1) * samples]
    sum_ref[home] = sum_ref[home] + jnp.concatenate(out, axis=0)


def field_of(table_ref, slots_ref, first, rows):
    return jnp.concatenate([slots_ref[table_ref[0, first + i]][:rows] for i in range(2)], axis=1)


def product(field, tile):
    return jnp.dot(field, tile, preferred_element_type=f32)


def multiply(table_ref, stage, slots_ref, even_ref, odd_ref, sum_ref):
    blocks, rows = sum_ref.shape[:2]
    count, home_of, first_of = duos_of(table_ref, stage, blocks)

    def both(turn, carry):
        duo = 2 * turn
        odd = jnp.where(duo + 1 < count, turn, 0)
        first = product(field_of(table_ref, slots_ref, first_of(duo), rows), even_ref[turn])
        second = product(field_of(table_ref, slots_ref, first_of(duo + 1), rows), odd_ref[odd])
        add_product(sum_ref, home_of(duo), first)
        add_product(sum_ref, jnp.minimum(home_of(duo + 1), blocks - 1), second)
        return carry

    lax.fori_loop(0, (count + 1) >> 1, both, 0)


def build(table_ref, stage, own_ref, slots_ref, even_ref, odd_ref, sum_ref, turn_even, turn_odd):
    blocks, rows = sum_ref.shape[:2]
    count, home_of, first_of = duos_of(table_ref, stage, blocks)
    odd_ref[0] = jnp.zeros(odd_ref.shape[1:], bf16)

    def prepare(duo, columns_ref):
        first = first_of(duo)
        columns_ref[:, :8] = turn_positions(slots_ref, table_ref[0, first], table_ref[0, first + 1], rows)

    def consume(duo, tile, index):
        field = field_of(table_ref, slots_ref, first_of(duo), rows)
        add_product(sum_ref, jnp.minimum(home_of(duo), blocks - 1), product(field, tile[index]))

    def make(duo, columns_ref, tile, index):
        place = position_of(own_ref, home_of(duo), rows)
        for i in range(2):
            make_tile(place, columns_ref, tile, index, i)

    def both(turn, spare):
        duo = 2 * turn
        full = duo + 1 < count
        make(duo, turn_even, even_ref, turn)
        prepare(duo + 1, turn_odd)
        consume(jnp.where(turn == 0, count, duo - 1), odd_ref, spare)

        @pl.when(full)
        def _():
            make(duo + 1, turn_odd, odd_ref, turn)
            prepare(duo + 2, turn_even)
            consume(duo, even_ref, turn)

        @pl.when(jnp.logical_not(full))
        def _():
            consume(duo, even_ref, turn)

        return jnp.where(full, turn, spare)

    prepare(0, turn_even)
    spare = lax.fori_loop(0, (count + 1) >> 1, both, 0)
    consume(jnp.where(count % 2 == 0, jnp.maximum(count - 1, 0), count), odd_ref, spare)


def new_field(block, mask_ref, sum_ref, old_ref):
    return sum_ref[block] * mask_ref[block, :1] - old_ref[block]


def stage_kernel(stage, building, moments, *refs):
    refs = list(refs)
    table_ref, own_ref = refs.pop(0), refs.pop(0) if building else None
    tiles = None if building else (refs.pop(0), refs.pop(0))
    before_ref = refs.pop(0) if stage else None
    last = stage == 2
    mask_ref = refs.pop(0) if last else None
    old = [refs.pop(0) for _ in range(3 if moments else 1)] if last else []
    columns = [refs.pop(), refs.pop()] if building else []
    sum_ref = refs.pop() if last else None
    slots_ref = refs.pop()
    outs = [refs.pop() for _ in range(1 if moments or not last else 2)][::-1]
    if building:
        tiles = [refs.pop(), refs.pop()][::-1]
    gather_slots(refs, slots_ref)
    if not last:
        sum_ref = outs[0]
    sum_ref[...] = before_ref[...] if stage else jnp.zeros_like(sum_ref)
    if building:
        build(table_ref, stage, own_ref, slots_ref, *tiles, sum_ref, *columns)
    else:
        multiply(table_ref, stage, slots_ref, *tiles, sum_ref)
    if moments:
        take_moments(mask_ref, sum_ref, *old, outs[0])
    elif last:
        for block in range(sum_ref.shape[0]):
            new = new_field(block, mask_ref, sum_ref, old[0])
            outs[0][block] = new
            outs[1][block] = new.astype(bf16)


MOMENTS = ((0, 0), (0, 1), (1, 1), (1, 2), (2, 2), (2, 3))


def take_moments(mask_ref, sum_ref, x0_ref, x1_ref, x2_ref, moment_ref):
    blocks, rows, beads = x0_ref.shape
    samples = rows // 3
    lanes = moment_ref.shape[2]
    lane = lax.broadcasted_iota(jnp.int32, (samples, lanes), 1)
    row = lax.broadcasted_iota(jnp.int32, (samples, lanes), 0)
    sums = [0.0] * len(MOMENTS)
    for block in range(blocks):
        x = [x0_ref[block], x1_ref[block], x2_ref[block]]
        x.append(new_field(block, mask_ref, sum_ref, x2_ref))
        for k, (i, j) in enumerate(MOMENTS):
            both = x[i] * x[j]
            sums[k] = sums[k] + both[:samples] + both[samples : 2 * samples] + both[2 * samples :]
    grid = jnp.zeros((samples, lanes), f32)
    for k, value in enumerate(sums):
        value = jnp.sum(value, axis=1, keepdims=True)
        grid = jnp.where(lane == row + k * samples, value, grid)
    line = jnp.sum(grid, axis=0, keepdims=True)
    moment_ref[...] = jnp.broadcast_to(line[None], moment_ref.shape)


def inverse_symmetric(m):
    a, b, c, d, e, f = m
    ca, cb, cc = d * f - e * e, c * e - b * f, b * e - c * d
    scale = 1.0 / (a * ca + b * cb + c * cc)
    return (ca * scale, cb * scale, cc * scale, (a * f - c * c) * scale, (b * c - a * e) * scale, (a * d - b * b) * scale)


def final_kernel(moment_ref, x0_ref, x1_ref, x2_ref, out_ref):
    blocks, rows, beads = x0_ref.shape
    samples = rows // 3
    lanes = moment_ref.shape[2]
    lane = lax.broadcasted_iota(jnp.int32, (samples, lanes), 1)
    row = lax.broadcasted_iota(jnp.int32, (samples, lanes), 0)
    line = jnp.broadcast_to(jnp.sum(moment_ref[...], axis=0), (samples, lanes))
    m00, m01, m11, m12, m22, m23 = [
        jnp.broadcast_to(
            jnp.sum(jnp.where(lane == row + k * samples, line, 0.0), axis=1, keepdims=True), (samples, lanes)
        )
        for k in range(len(MOMENTS))
    ]
    norm_sq = m00 + epsilon
    start_norm = jnp.sqrt(norm_sq)
    inv_sq = 1.0 / norm_sq
    alpha1 = (m00 + m01) * inv_sq
    c = 1.0 - alpha1
    res_sq = (m11 + c * (2.0 * m01 + c * m00)) * inv_sq
    beta1 = jnp.sqrt(jnp.maximum(res_sq, 0.0) + epsilon)
    k2 = 1.0 / (start_norm * beta1)
    n11 = m11 + c * (2.0 * m01 + c * m00)
    n12 = m12 + c * (2.0 * m11 + c * m01)
    alpha2 = k2 * k2 * (n11 + n12)
    f1 = 1.0 + c - alpha2
    f0 = c - alpha2 * c - beta1 * beta1
    n22 = m22 + f1 * (2.0 * m12 + f1 * m11) + f0 * (2.0 * (m11 + f1 * m01) + f0 * m00)
    beta2 = jnp.sqrt(jnp.maximum(k2 * k2 * n22, 0.0) + epsilon)
    k3 = k2 / beta2
    n23 = m23 + f1 * (2.0 * m22 + f1 * m12) + f0 * (2.0 * (m12 + f1 * m11) + f0 * m01)
    alpha3 = k3 * k3 * (jnp.maximum(n22, 0.0) + n23)

    scale = (alpha1 + alpha2 + alpha3) / 3.0
    inv_scale = 1.0 / scale
    zero, one = jnp.zeros_like(scale), jnp.ones_like(scale)
    y = (alpha1 * inv_scale, beta1 * inv_scale, zero, alpha2 * inv_scale, beta2 * inv_scale, alpha3 * inv_scale)
    z = (one, zero, zero, one, zero, one)
    for _ in range(ROOT_ITERS):
        inv_z, inv_y = inverse_symmetric(z), inverse_symmetric(y)
        y = tuple(0.5 * (p + q) for p, q in zip(y, inv_z))
        z = tuple(0.5 * (p + q) for p, q in zip(z, inv_y))
    root_scale = jnp.sqrt(scale)
    r1, r2, r3 = root_scale * y[0], root_scale * y[1], root_scale * y[2]
    w2, w3 = start_norm * r2 * k2, start_norm * r3 * k3
    p0 = r1 + w2 * c + w3 * f0
    p1 = w2 + w3 * f1
    for block in range(blocks):
        for c in range(3):
            at = pl.ds(c * samples, samples)
            out = p0 * x0_ref[block, at] + p1 * x1_ref[block, at] + w3 * x2_ref[block, at]
            out_ref[0, 0, block, :, pl.ds(c * beads, beads)] = out


def call(kernel, outs, in_specs, scratch=(), limit=None, cost=None):
    return pl.pallas_call(
        kernel,
        out_shape=outs,
        in_specs=in_specs,
        out_specs=jax.tree.map(lambda _: VMEM, outs),
        scratch_shapes=list(scratch),
        compiler_params=pltpu.CompilerParams(vmem_limit_bytes=limit),
        cost_estimate=cost,
    )


def body(positions, block_fill, noise, pair_list, pair_count):
    blocks, beads = positions.shape[2], positions.shape[4]
    samples = noise.shape[3]
    rows = 3 * samples
    shape = (blocks, rows, beads)
    devices = lax.axis_size(AXES)
    columns = 2 if lax.axis_size("gx") == 2 else 3
    others = 1 if lax.axis_size("gy") == 2 else 2
    sides = 1 if lax.axis_size("gz") == 2 else 2
    slots = (columns * blocks, others * columns * blocks, sides * (1 + others) * columns)
    limit = 8 << 20

    x0, mask, packed = call(
        pack_kernel,
        (
            jax.ShapeDtypeStruct(shape, f32),
            jax.ShapeDtypeStruct((blocks, 8, beads), f32),
            jax.ShapeDtypeStruct((blocks, rows + 16, beads), bf16),
        ),
        [HBM] * 3,
        (
            pltpu.SMEM(block_fill.shape, jnp.int32),
            pltpu.VMEM(noise.shape, f32),
            pltpu.VMEM((1, 1, 3, blocks, beads), f32),
            pltpu.SemaphoreType.DMA((3,)),
        ),
        4 << 20,
    )(*[pltpu.with_memory_space_constraint(a, pltpu.HBM) for a in (block_fill, noise, jnp.swapaxes(positions, 2, 3))])
    table = pair_table(pair_list, pair_count, blocks, slots)
    field, sent = jax.ShapeDtypeStruct(shape, f32), jax.ShapeDtypeStruct(shape, bf16)
    capacity = (pair_list.shape[4] + blocks) // 4 + 1
    tile = jax.ShapeDtypeStruct((capacity, 2 * beads, len(PLACES) * beads), bf16)
    total = pltpu.VMEM(shape, f32)
    moment = jax.ShapeDtypeStruct((devices, 1, 128), f32)
    cost = pl.CostEstimate(flops=10**8, bytes_accessed=10**7, transcendentals=0)

    def apply(vector, tiles, olds):
        building, moments = not tiles, len(olds) == 3

        def stage(table, index, given, result):
            last = index == 2
            outs = (moment,) if last and moments else (field, sent) if last else (field,)
            scratch = [pltpu.VMEM((slots[index] + 1,) + given[0].shape[1:], bf16)]
            scratch += [total] * last + [pltpu.VMEM((beads, 128), f32)] * (2 * building)
            args = [packed] if building else list(tiles[index])
            args += ([result] if index else []) + ([mask] + olds if last else []) + given
            result = call(
                functools.partial(stage_kernel, index, building, last and moments),
                (tile, tile) * building + outs,
                [SMEM] + [VMEM] * len(args),
                scratch,
                limit,
                None if last else cost,
            )(table, *args)
            if building:
                tiles.append(result[:2])
                result = result[2:]
            return result if last and not moments else result[0]

        at_once = lax.axis_size(("gx", "gy")) <= 8
        return spread(vector, table, stage, at_once)

    tiles = []
    x1, send = apply(packed, tiles, [x0])
    x2, send = apply(send, tiles, [x1])
    moments = apply(send, tiles, [x0, x1, x2])
    moments = lax.all_to_all(moments, AXES, 0, 0)
    return call(final_kernel, jax.ShapeDtypeStruct(noise.shape, f32), [VMEM] * 4, (), 4 << 20)(moments, x0, x1, x2)


def solution(mesh):
    block = P("gx", "gy", "gz", None, None)
    cell = P("gx", "gy", "gz")
    return jax.shard_map(
        body, mesh=mesh, in_specs=(block, cell, block, block, cell), out_specs=block, check_vma=False
    )
```

```python
import functools

import jax
import jax.numpy as jnp
from jax import lax
from jax.experimental import pallas as pl
from jax.experimental.pallas import tpu as pltpu
from jax.sharding import PartitionSpec as P

ITERS = 3
ROOT_ITERS = 12
CHUNK = 16

radius = 0.08
floor_sq = 0.0001
epsilon = 1e-06

AXES = ("gx", "gy", "gz")
VMEM = pl.BlockSpec(memory_space=pltpu.VMEM)
HBM = pl.BlockSpec(memory_space=pltpu.HBM)
SMEM = pl.BlockSpec(memory_space=pltpu.SMEM)
f32 = jnp.float32
bf16 = jnp.bfloat16
PLACES = ((0, 0), (0, 1), (0, 2), (1, 1), (1, 2), (2, 2))


def matching(count, parity):
    pairs = []
    for i in range(parity, count - 1, 2):
        pairs += [(i, i + 1), (i + 1, i)]
    return pairs


def swaps(axis, first, second):
    count = lax.axis_size(axis)
    got = [lax.ppermute(first, axis, matching(count, 0))]
    if count > 2:
        got.append(lax.ppermute(second, axis, matching(count, 1)))
    return got


def plane_exchange(field):
    plane = ("gx", "gy")
    size_x, size_y = [lax.axis_size(axis) for axis in plane]
    got = lax.all_to_all(jnp.broadcast_to(field[None], (size_x * size_y,) + field.shape), plane, 0, 0)
    x, y = [lax.axis_index(axis) for axis in plane]

    def partners(index, count):
        even, odd = index + 1 - 2 * (index % 2), index - 1 + 2 * (index % 2)
        return [index, jnp.minimum(even, count - 1)] + [jnp.clip(odd, 0, count - 1)] * (count > 2)

    rows = [
        jnp.stack([lax.dynamic_index_in_dim(got, i * size_y + j, 0, False) for i in partners(x, size_x)])
        for j in partners(y, size_y)
    ]
    return rows[0], rows[1:]


def spread(field, table, stage, at_once):
    shape = (-1,) + field.shape[1:]
    if at_once:
        columns, others = plane_exchange(field)
    else:
        columns = jnp.stack([field] + swaps("gx", field, field))
        columns, table = lax.optimization_barrier((columns, table))
        others = swaps("gy", columns, columns)
    rows = [part.reshape(shape) for part in [columns] + others]
    result = None if at_once else stage(table, 0, rows[:1], None)
    odd = lax.axis_index("gz") % 2 == 1
    low = jnp.concatenate([part[:, 0] for part in [columns] + others])
    high = jnp.concatenate([part[:, field.shape[0] - 1] for part in [columns] + others])
    low, high = jnp.where(odd, low, high), jnp.where(odd, high, low)
    if not at_once:
        low, high, result = lax.optimization_barrier((low, high, result))
    far = swaps("gz", low, high)
    result = stage(table, 1, rows if at_once else rows[1:], result)
    return stage(table, 2, far, result)


def table_kernel(sizes, slots, width, at_once, blocks, count_ref, list_hbm, table_ref, list_ref, sem):
    copy = pltpu.make_async_copy(list_hbm, list_ref, sem)
    copy.start()
    sets = len(slots) * blocks
    segment = table_ref.shape[1] // sets
    for i in range(sets):
        table_ref[1, i] = 0
    odd = [lax.rem(lax.axis_index(axis), 2) == 1 for axis in AXES]

    def partner(axis, step):
        if sizes[axis] == 2:
            return jnp.where(step == 0, 0, 1)
        return jnp.where(step == 0, 0, jnp.where((step < 0) == odd[axis], 1, 2))

    def enter(t, carry):
        home, code = list_ref[0, 0, 0, 0, t], list_ref[0, 0, 1, 0, t]
        plane, third = (code * 57) >> 9, (code * 43) >> 7
        x, y = partner(0, plane - 1), partner(1, third - 3 * plane - 1)
        z = home + code - 3 * third - 1
        far = (z < 0) | (z >= blocks)
        side = partner(2, jnp.where(z < 0, -1, 1)) - 1
        row = y if at_once else jnp.maximum(y - 1, 0)
        slot = (row * width + x) * blocks + z
        slot = jnp.where(far, side * (slots[2] // (1 if sizes[2] == 2 else 2)) + y * width + x, slot)
        at = jnp.where(far, 2, 1 if at_once else jnp.minimum(y, 1)) * blocks + home
        place = table_ref[1, at]
        table_ref[1, at] = place + 1
        table_ref[0, at * segment + place] = slot
        return carry

    copy.wait()
    lax.fori_loop(0, count_ref[0, 0, 0], enter, 0)
    for stage, empty in enumerate(slots):
        for block in range(blocks):
            at = stage * blocks + block
            end = at * segment + table_ref[1, at]
            for i in range(3):
                table_ref[0, end + i] = empty


def pair_table(pair_list, pair_count, blocks, slots, width, at_once):
    segment = -(-(pair_list.shape[4] + 3) // 2) * 2
    sizes = [lax.axis_size(axis) for axis in AXES]
    pair_list = pltpu.with_memory_space_constraint(jnp.swapaxes(pair_list, 2, 3), pltpu.HBM)
    return pl.pallas_call(
        functools.partial(table_kernel, sizes, slots, width, at_once, blocks),
        out_shape=jax.ShapeDtypeStruct((2, len(slots) * blocks * segment), jnp.int32),
        in_specs=[SMEM, HBM],
        out_specs=SMEM,
        scratch_shapes=[pltpu.SMEM(pair_list.shape, jnp.int32), pltpu.SemaphoreType.DMA],
        compiler_params=pltpu.CompilerParams(vmem_limit_bytes=1 << 20),
        cost_estimate=pl.CostEstimate(flops=10**6, bytes_accessed=10**6, transcendentals=0),
    )(pair_count, pair_list)


def duos_of(table_ref, stage, blocks):
    segment = table_ref.shape[1] // (3 * blocks)
    counts = [(table_ref[1, stage * blocks + block] + 1) >> 1 for block in range(blocks)]
    ends = [sum(counts[: block + 1]) for block in range(blocks)]

    def home_of(duo):
        return sum([jnp.where(duo >= end, 1, 0) for end in ends[:-1]], 0)

    def first_of(duo):
        skip = [jnp.where(duo >= ends[i], segment - 2 * counts[i], 0) for i in range(blocks - 1)]
        return stage * blocks * segment + 2 * duo + sum(skip)

    return ends[-1], home_of, first_of


def pack_kernel(fill_hbm, noise_hbm, pos_hbm, start_ref, mask_ref, pack_ref, fill_ref, noise_ref, pos_ref, sems):
    pairs = ((fill_hbm, fill_ref), (noise_hbm, noise_ref), (pos_hbm, pos_ref))
    copies = [pltpu.make_async_copy(a, b, sems.at[i]) for i, (a, b) in enumerate(pairs)]
    for copy in copies:
        copy.start()
    for copy in copies:
        copy.wait()
    blocks, samples, width = noise_ref.shape[2:]
    beads = width // 3
    row = lax.broadcasted_iota(jnp.int32, (16, beads), 0)
    for block in range(blocks):
        mask = (lax.broadcasted_iota(jnp.int32, (8, beads), 1) < fill_ref[0, 0, block]).astype(f32)
        mask_ref[block] = mask
        noise = [noise_ref[0, 0, block, :, pl.ds(c * beads, beads)] for c in range(3)]
        start = jnp.concatenate([part * mask[:1] for part in noise], axis=0)
        start_ref[block] = start
        place = jnp.zeros((16, beads), f32)
        for c in range(3):
            pos = pos_ref[0, 0, c, pl.ds(block, 1)]
            high = pos.astype(bf16).astype(f32)
            rest = pos - high
            mid = rest.astype(bf16).astype(f32)
            for i, piece in ((0, high), (8, mid), (3, rest - mid)):
                place = jnp.where(row == i + c, piece, place)
        pack_ref[block] = jnp.concatenate([start, place], axis=0).astype(bf16)


def gather_slots(parts, slots_ref):
    count = parts[0].shape[0]
    for i, part in enumerate(parts):
        slots_ref[pl.ds(i * count, count)] = part[...]
    slots_ref[len(parts) * count] = jnp.zeros(slots_ref.shape[1:], bf16)


def position_of(slots_ref, slot, field_rows):
    rows = slots_ref[slot].astype(f32)[field_rows:]
    return rows[:8] + rows[8:] + pltpu.roll(rows[:8], 5, 0)


def turn_positions(slots_ref, first, second, field_rows):
    first = position_of(slots_ref, first, field_rows)
    second = pltpu.roll(position_of(slots_ref, second, field_rows), 3, 0)
    row = lax.broadcasted_iota(jnp.int32, first.shape, 0)
    return jnp.transpose(jnp.where(row < 3, first, second))


def make_tile(home, turned_ref, tiles_ref, pair, half):
    beads = home.shape[1]
    base = half * beads
    for first in range(0, beads, CHUNK):
        turned = turned_ref[pl.ds(first, CHUNK)]
        d = [turned[:, 3 * half + c : 3 * half + c + 1] - home[c : c + 1] for c in range(3)]
        dist_sq = d[0] * d[0] + d[1] * d[1] + d[2] * d[2]
        root = lax.rsqrt(jnp.maximum(dist_sq, 1e-30))
        distance = dist_sq * root
        inv_root = jnp.minimum(root, floor_sq**-0.5)
        inverse_sq = inv_root * inv_root
        far = (0.75 * radius) * inv_root
        far_two = (2.0 * radius * radius) * (far * inverse_sq)
        apart = dist_sq >= 4.0 * radius * radius
        isotropic = jnp.where(apart, far + far_two * (1.0 / 3.0), 1.0 - (9.0 / 32.0 / radius) * distance)
        dyadic = jnp.where(apart, far - far_two, (3.0 / 32.0 / radius) * distance) * inverse_sq
        scaled = [dyadic * d[c] for c in range(3)]
        entries = []
        for c, e in PLACES:
            entry = scaled[c] * d[e]
            entries.append(entry + isotropic if c == e else entry)
        tiles_ref[pair, pl.ds(base + first, CHUNK)] = jnp.concatenate(entries, axis=1).astype(bf16)


def add_product(sum_ref, home, product):
    rows, beads = sum_ref.shape[1:]
    samples = rows // 3
    out = [0.0] * 3
    for k, (c, e) in enumerate(PLACES):
        column = product[:, k * beads : (k + 1) * beads]
        out[c] = out[c] + column[e * samples : (e + 1) * samples]
        if c != e:
            out[e] = out[e] + column[c * samples : (c + 1) * samples]
    sum_ref[home] = sum_ref[home] + jnp.concatenate(out, axis=0)


def field_of(table_ref, slots_ref, first, rows):
    return jnp.concatenate([slots_ref[table_ref[0, first + i]][:rows] for i in range(2)], axis=1)


def product(field, tile):
    return jnp.dot(field, tile, preferred_element_type=f32)


def multiply(table_ref, stage, slots_ref, even_ref, odd_ref, sum_ref):
    blocks, rows = sum_ref.shape[:2]
    count, home_of, first_of = duos_of(table_ref, stage, blocks)

    def both(turn, carry):
        duo = 2 * turn
        odd = jnp.where(duo + 1 < count, turn, 0)
        first = product(field_of(table_ref, slots_ref, first_of(duo), rows), even_ref[turn])
        second = product(field_of(table_ref, slots_ref, first_of(duo + 1), rows), odd_ref[odd])
        add_product(sum_ref, home_of(duo), first)
        add_product(sum_ref, jnp.minimum(home_of(duo + 1), blocks - 1), second)
        return carry

    lax.fori_loop(0, (count + 1) >> 1, both, 0)


def build(table_ref, stage, own_ref, slots_ref, even_ref, odd_ref, sum_ref, turn_even, turn_odd):
    blocks, rows = sum_ref.shape[:2]
    count, home_of, first_of = duos_of(table_ref, stage, blocks)
    odd_ref[0] = jnp.zeros(odd_ref.shape[1:], bf16)

    def prepare(duo, columns_ref):
        first = first_of(duo)
        columns_ref[:, :8] = turn_positions(slots_ref, table_ref[0, first], table_ref[0, first + 1], rows)

    def consume(duo, tile, index):
        field = field_of(table_ref, slots_ref, first_of(duo), rows)
        add_product(sum_ref, jnp.minimum(home_of(duo), blocks - 1), product(field, tile[index]))

    def make(duo, columns_ref, tile, index):
        place = position_of(own_ref, home_of(duo), rows)
        for i in range(2):
            make_tile(place, columns_ref, tile, index, i)

    def both(turn, spare):
        duo = 2 * turn
        full = duo + 1 < count
        make(duo, turn_even, even_ref, turn)
        prepare(duo + 1, turn_odd)
        consume(jnp.where(turn == 0, count, duo - 1), odd_ref, spare)

        @pl.when(full)
        def _():
            make(duo + 1, turn_odd, odd_ref, turn)
            prepare(duo + 2, turn_even)
            consume(duo, even_ref, turn)

        @pl.when(jnp.logical_not(full))
        def _():
            consume(duo, even_ref, turn)

        return jnp.where(full, turn, spare)

    prepare(0, turn_even)
    spare = lax.fori_loop(0, (count + 1) >> 1, both, 0)
    consume(jnp.where(count % 2 == 0, jnp.maximum(count - 1, 0), count), odd_ref, spare)


def new_field(block, mask_ref, sum_ref, old_ref):
    return sum_ref[block] * mask_ref[block, :1] - old_ref[block]


def stage_kernel(stage, begins, building, moments, *refs):
    refs = list(refs)
    table_ref, own_ref = refs.pop(0), refs.pop(0) if building else None
    tiles = None if building else (refs.pop(0), refs.pop(0))
    before_ref = None if begins else refs.pop(0)
    last = stage == 2
    mask_ref = refs.pop(0) if last else None
    old = [refs.pop(0) for _ in range(3 if moments else 1)] if last else []
    columns = [refs.pop(), refs.pop()] if building else []
    sum_ref = refs.pop() if last else None
    slots_ref = refs.pop()
    outs = [refs.pop() for _ in range(1 if moments or not last else 2)][::-1]
    if building:
        tiles = [refs.pop(), refs.pop()][::-1]
    gather_slots(refs, slots_ref)
    if not last:
        sum_ref = outs[0]
    sum_ref[...] = jnp.zeros_like(sum_ref) if begins else before_ref[...]
    if building:
        build(table_ref, stage, own_ref, slots_ref, *tiles, sum_ref, *columns)
    else:
        multiply(table_ref, stage, slots_ref, *tiles, sum_ref)
    if moments:
        take_moments(mask_ref, sum_ref, *old, outs[0])
    elif last:
        for block in range(sum_ref.shape[0]):
            new = new_field(block, mask_ref, sum_ref, old[0])
            outs[0][block] = new
            outs[1][block] = new.astype(bf16)


MOMENTS = ((0, 0), (0, 1), (1, 1), (1, 2), (2, 2), (2, 3))


def take_moments(mask_ref, sum_ref, x0_ref, x1_ref, x2_ref, moment_ref):
    blocks, rows, beads = x0_ref.shape
    samples = rows // 3
    lanes = moment_ref.shape[2]
    lane = lax.broadcasted_iota(jnp.int32, (samples, lanes), 1)
    row = lax.broadcasted_iota(jnp.int32, (samples, lanes), 0)
    sums = [0.0] * len(MOMENTS)
    for block in range(blocks):
        x = [x0_ref[block], x1_ref[block], x2_ref[block]]
        x.append(new_field(block, mask_ref, sum_ref, x2_ref))
        for k, (i, j) in enumerate(MOMENTS):
            both = x[i] * x[j]
            sums[k] = sums[k] + both[:samples] + both[samples : 2 * samples] + both[2 * samples :]
    grid = jnp.zeros((samples, lanes), f32)
    for k, value in enumerate(sums):
        value = jnp.sum(value, axis=1, keepdims=True)
        grid = jnp.where(lane == row + k * samples, value, grid)
    line = jnp.sum(grid, axis=0, keepdims=True)
    moment_ref[...] = jnp.broadcast_to(line[None], moment_ref.shape)


def inverse_symmetric(m):
    a, b, c, d, e, f = m
    ca, cb, cc = d * f - e * e, c * e - b * f, b * e - c * d
    scale = 1.0 / (a * ca + b * cb + c * cc)
    return (ca * scale, cb * scale, cc * scale, (a * f - c * c) * scale, (b * c - a * e) * scale, (a * d - b * b) * scale)


def final_kernel(moment_ref, x0_ref, x1_ref, x2_ref, out_ref):
    blocks, rows, beads = x0_ref.shape
    samples = rows // 3
    lanes = moment_ref.shape[2]
    lane = lax.broadcasted_iota(jnp.int32, (samples, lanes), 1)
    row = lax.broadcasted_iota(jnp.int32, (samples, lanes), 0)
    line = jnp.broadcast_to(jnp.sum(moment_ref[...], axis=0), (samples, lanes))
    m00, m01, m11, m12, m22, m23 = [
        jnp.broadcast_to(
            jnp.sum(jnp.where(lane == row + k * samples, line, 0.0), axis=1, keepdims=True), (samples, lanes)
        )
        for k in range(len(MOMENTS))
    ]
    norm_sq = m00 + epsilon
    start_norm = jnp.sqrt(norm_sq)
    inv_sq = 1.0 / norm_sq
    alpha1 = (m00 + m01) * inv_sq
    c = 1.0 - alpha1
    res_sq = (m11 + c * (2.0 * m01 + c * m00)) * inv_sq
    beta1 = jnp.sqrt(jnp.maximum(res_sq, 0.0) + epsilon)
    k2 = 1.0 / (start_norm * beta1)
    n11 = m11 + c * (2.0 * m01 + c * m00)
    n12 = m12 + c * (2.0 * m11 + c * m01)
    alpha2 = k2 * k2 * (n11 + n12)
    f1 = 1.0 + c - alpha2
    f0 = c - alpha2 * c - beta1 * beta1
    n22 = m22 + f1 * (2.0 * m12 + f1 * m11) + f0 * (2.0 * (m11 + f1 * m01) + f0 * m00)
    beta2 = jnp.sqrt(jnp.maximum(k2 * k2 * n22, 0.0) + epsilon)
    k3 = k2 / beta2
    n23 = m23 + f1 * (2.0 * m22 + f1 * m12) + f0 * (2.0 * (m12 + f1 * m11) + f0 * m01)
    alpha3 = k3 * k3 * (jnp.maximum(n22, 0.0) + n23)

    scale = (alpha1 + alpha2 + alpha3) / 3.0
    inv_scale = 1.0 / scale
    zero, one = jnp.zeros_like(scale), jnp.ones_like(scale)
    y = (alpha1 * inv_scale, beta1 * inv_scale, zero, alpha2 * inv_scale, beta2 * inv_scale, alpha3 * inv_scale)
    z = (one, zero, zero, one, zero, one)
    for _ in range(ROOT_ITERS):
        inv_z, inv_y = inverse_symmetric(z), inverse_symmetric(y)
        y = tuple(0.5 * (p + q) for p, q in zip(y, inv_z))
        z = tuple(0.5 * (p + q) for p, q in zip(z, inv_y))
    root_scale = jnp.sqrt(scale)
    r1, r2, r3 = root_scale * y[0], root_scale * y[1], root_scale * y[2]
    w2, w3 = start_norm * r2 * k2, start_norm * r3 * k3
    p0 = r1 + w2 * c + w3 * f0
    p1 = w2 + w3 * f1
    for block in range(blocks):
        for c in range(3):
            at = pl.ds(c * samples, samples)
            out = p0 * x0_ref[block, at] + p1 * x1_ref[block, at] + w3 * x2_ref[block, at]
            out_ref[0, 0, block, :, pl.ds(c * beads, beads)] = out


def call(kernel, outs, in_specs, scratch=(), limit=None, cost=None):
    return pl.pallas_call(
        kernel,
        out_shape=outs,
        in_specs=in_specs,
        out_specs=jax.tree.map(lambda _: VMEM, outs),
        scratch_shapes=list(scratch),
        compiler_params=pltpu.CompilerParams(vmem_limit_bytes=limit),
        cost_estimate=cost,
    )


def body(positions, block_fill, noise, pair_list, pair_count):
    blocks, beads = positions.shape[2], positions.shape[4]
    samples = noise.shape[3]
    rows = 3 * samples
    shape = (blocks, rows, beads)
    devices = lax.axis_size(AXES)
    columns = 2 if lax.axis_size("gx") == 2 else 3
    others = 1 if lax.axis_size("gy") == 2 else 2
    sides = 1 if lax.axis_size("gz") == 2 else 2
    at_once = lax.axis_size(("gx", "gy")) <= 8
    middle = others + 1 if at_once else others
    slots = (columns * blocks, middle * columns * blocks, sides * (1 + others) * columns)
    limit = 8 << 20

    x0, mask, packed = call(
        pack_kernel,
        (
            jax.ShapeDtypeStruct(shape, f32),
            jax.ShapeDtypeStruct((blocks, 8, beads), f32),
            jax.ShapeDtypeStruct((blocks, rows + 16, beads), bf16),
        ),
        [HBM] * 3,
        (
            pltpu.SMEM(block_fill.shape, jnp.int32),
            pltpu.VMEM(noise.shape, f32),
            pltpu.VMEM((1, 1, 3, blocks, beads), f32),
            pltpu.SemaphoreType.DMA((3,)),
        ),
        4 << 20,
    )(*[pltpu.with_memory_space_constraint(a, pltpu.HBM) for a in (block_fill, noise, jnp.swapaxes(positions, 2, 3))])
    table = pair_table(pair_list, pair_count, blocks, slots, columns, at_once)
    field, sent = jax.ShapeDtypeStruct(shape, f32), jax.ShapeDtypeStruct(shape, bf16)
    capacity = (pair_list.shape[4] + blocks) // 4 + 1
    tile = jax.ShapeDtypeStruct((capacity, 2 * beads, len(PLACES) * beads), bf16)
    total = pltpu.VMEM(shape, f32)
    moment = jax.ShapeDtypeStruct((devices, 1, 128), f32)
    cost = pl.CostEstimate(flops=10**8, bytes_accessed=10**7, transcendentals=0)

    def apply(vector, tiles, olds):
        building, moments = not tiles, len(olds) == 3

        def stage(table, index, given, result):
            last = index == 2
            outs = (moment,) if last and moments else (field, sent) if last else (field,)
            scratch = [pltpu.VMEM((slots[index] + 1,) + given[0].shape[1:], bf16)]
            scratch += [total] * last + [pltpu.VMEM((beads, 128), f32)] * (2 * building)
            args = [packed] if building else list(tiles[index])
            args += ([] if result is None else [result]) + ([mask] + olds if last else []) + given
            result = call(
                functools.partial(stage_kernel, index, result is None, building, last and moments),
                (tile, tile) * building + outs,
                [SMEM] + [VMEM] * len(args),
                scratch,
                limit,
                None if last else cost,
            )(table, *args)
            if building:
                tiles[index] = result[:2]
                result = result[2:]
            return result if last and not moments else result[0]

        return spread(vector, table, stage, at_once)

    tiles = {}
    x1, send = apply(packed, tiles, [x0])
    x2, send = apply(send, tiles, [x1])
    moments = apply(send, tiles, [x0, x1, x2])
    moments = lax.all_to_all(moments, AXES, 0, 0)
    return call(final_kernel, jax.ShapeDtypeStruct(noise.shape, f32), [VMEM] * 4, (), 4 << 20)(moments, x0, x1, x2)


def solution(mesh):
    block = P("gx", "gy", "gz", None, None)
    cell = P("gx", "gy", "gz")
    return jax.shard_map(
        body, mesh=mesh, in_specs=(block, cell, block, block, cell), out_specs=block, check_vma=False
    )
```

```python
import functools

import jax
import jax.numpy as jnp
from jax import lax
from jax.experimental import pallas as pl
from jax.experimental.pallas import tpu as pltpu
from jax.sharding import PartitionSpec as P

ITERS = 3
ROOT_ITERS = 12
CHUNK = 16

radius = 0.08
floor_sq = 0.0001
epsilon = 1e-06

AXES = ("gx", "gy", "gz")
VMEM = pl.BlockSpec(memory_space=pltpu.VMEM)
HBM = pl.BlockSpec(memory_space=pltpu.HBM)
SMEM = pl.BlockSpec(memory_space=pltpu.SMEM)
f32 = jnp.float32
bf16 = jnp.bfloat16
PLACES = ((0, 0), (0, 1), (0, 2), (1, 1), (1, 2), (2, 2))


def matching(count, parity):
    pairs = []
    for i in range(parity, count - 1, 2):
        pairs += [(i, i + 1), (i + 1, i)]
    return pairs


def swaps(axis, first, second):
    count = lax.axis_size(axis)
    got = [lax.ppermute(first, axis, matching(count, 0))]
    if count > 2:
        got.append(lax.ppermute(second, axis, matching(count, 1)))
    return got


def plane_exchange(field):
    plane = ("gx", "gy")
    size_x, size_y = [lax.axis_size(axis) for axis in plane]
    got = lax.all_to_all(jnp.broadcast_to(field[None], (size_x * size_y,) + field.shape), plane, 0, 0)
    x, y = [lax.axis_index(axis) for axis in plane]

    def partners(index, count):
        even, odd = index + 1 - 2 * (index % 2), index - 1 + 2 * (index % 2)
        return [index, jnp.minimum(even, count - 1)] + [jnp.clip(odd, 0, count - 1)] * (count > 2)

    rows = [
        jnp.stack([lax.dynamic_index_in_dim(got, i * size_y + j, 0, False) for i in partners(x, size_x)])
        for j in partners(y, size_y)
    ]
    return rows[0], rows[1:]


def spread(field, table, stage, at_once):
    shape = (-1,) + field.shape[1:]
    if at_once:
        columns, others = plane_exchange(field)
    else:
        columns = jnp.stack([field] + swaps("gx", field, field))
        columns, table = lax.optimization_barrier((columns, table))
        others = swaps("gy", columns, columns)
    rows = [part.reshape(shape) for part in [columns] + others]
    result = None if at_once else stage(table, 0, rows[:1], None)
    odd = lax.axis_index("gz") % 2 == 1
    low = jnp.concatenate([part[:, 0] for part in [columns] + others])
    high = jnp.concatenate([part[:, field.shape[0] - 1] for part in [columns] + others])
    low, high = jnp.where(odd, low, high), jnp.where(odd, high, low)
    if not at_once:
        low, high, result = lax.optimization_barrier((low, high, result))
    far = swaps("gz", low, high)
    result = stage(table, 1, rows if at_once else rows[1:], result)
    return stage(table, 2, far, result)


def table_kernel(sizes, slots, width, at_once, blocks, count_ref, list_hbm, table_ref, list_ref, sem):
    copy = pltpu.make_async_copy(list_hbm, list_ref, sem)
    copy.start()
    sets = len(slots) * blocks
    segment = table_ref.shape[1] // sets
    for i in range(sets):
        table_ref[1, i] = 0
    odd = [lax.rem(lax.axis_index(axis), 2) == 1 for axis in AXES]

    def partner(axis, step):
        if sizes[axis] == 2:
            return jnp.where(step == 0, 0, 1)
        return jnp.where(step == 0, 0, jnp.where((step < 0) == odd[axis], 1, 2))

    def enter(t, carry):
        home, code = list_ref[0, 0, 0, 0, t], list_ref[0, 0, 1, 0, t]
        plane, third = (code * 57) >> 9, (code * 43) >> 7
        x, y = partner(0, plane - 1), partner(1, third - 3 * plane - 1)
        z = home + code - 3 * third - 1
        far = (z < 0) | (z >= blocks)
        side = partner(2, jnp.where(z < 0, -1, 1)) - 1
        row = y if at_once else jnp.maximum(y - 1, 0)
        slot = (row * width + x) * blocks + z
        slot = jnp.where(far, side * (slots[2] // (1 if sizes[2] == 2 else 2)) + y * width + x, slot)
        at = jnp.where(far, 2, 1 if at_once else jnp.minimum(y, 1)) * blocks + home
        place = table_ref[1, at]
        table_ref[1, at] = place + 1
        table_ref[0, at * segment + place] = slot
        return carry

    copy.wait()
    lax.fori_loop(0, count_ref[0, 0, 0], enter, 0)
    for stage, empty in enumerate(slots):
        for block in range(blocks):
            at = stage * blocks + block
            end = at * segment + table_ref[1, at]
            for i in range(3):
                table_ref[0, end + i] = empty


def pair_table(pair_list, pair_count, blocks, slots, width, at_once):
    segment = -(-(pair_list.shape[4] + 3) // 2) * 2
    sizes = [lax.axis_size(axis) for axis in AXES]
    pair_list = pltpu.with_memory_space_constraint(jnp.swapaxes(pair_list, 2, 3), pltpu.HBM)
    return pl.pallas_call(
        functools.partial(table_kernel, sizes, slots, width, at_once, blocks),
        out_shape=jax.ShapeDtypeStruct((2, len(slots) * blocks * segment), jnp.int32),
        in_specs=[SMEM, HBM],
        out_specs=SMEM,
        scratch_shapes=[pltpu.SMEM(pair_list.shape, jnp.int32), pltpu.SemaphoreType.DMA],
        compiler_params=pltpu.CompilerParams(vmem_limit_bytes=1 << 20),
        cost_estimate=pl.CostEstimate(flops=10**6, bytes_accessed=10**6, transcendentals=0),
    )(pair_count, pair_list)


def duos_of(table_ref, stage, blocks):
    segment = table_ref.shape[1] // (3 * blocks)
    counts = [(table_ref[1, stage * blocks + block] + 1) >> 1 for block in range(blocks)]
    ends = [sum(counts[: block + 1]) for block in range(blocks)]

    def home_of(duo):
        return sum([jnp.where(duo >= end, 1, 0) for end in ends[:-1]], 0)

    def first_of(duo):
        skip = [jnp.where(duo >= ends[i], segment - 2 * counts[i], 0) for i in range(blocks - 1)]
        return stage * blocks * segment + 2 * duo + sum(skip)

    return ends[-1], home_of, first_of


def pack_kernel(fill_hbm, noise_hbm, pos_hbm, start_ref, mask_ref, pack_ref, fill_ref, noise_ref, pos_ref, sems):
    pairs = ((fill_hbm, fill_ref), (noise_hbm, noise_ref), (pos_hbm, pos_ref))
    copies = [pltpu.make_async_copy(a, b, sems.at[i]) for i, (a, b) in enumerate(pairs)]
    for copy in copies:
        copy.start()
    for copy in copies:
        copy.wait()
    blocks, samples, width = noise_ref.shape[2:]
    beads = width // 3
    row = lax.broadcasted_iota(jnp.int32, (16, beads), 0)
    for block in range(blocks):
        mask = (lax.broadcasted_iota(jnp.int32, (8, beads), 1) < fill_ref[0, 0, block]).astype(f32)
        mask_ref[block] = mask
        noise = [noise_ref[0, 0, block, :, pl.ds(c * beads, beads)] for c in range(3)]
        start = jnp.concatenate([part * mask[:1] for part in noise], axis=0)
        start_ref[block] = start
        place = jnp.zeros((16, beads), f32)
        for c in range(3):
            pos = pos_ref[0, 0, c, pl.ds(block, 1)]
            high = pos.astype(bf16).astype(f32)
            rest = pos - high
            mid = rest.astype(bf16).astype(f32)
            for i, piece in ((0, high), (8, mid), (3, rest - mid)):
                place = jnp.where(row == i + c, piece, place)
        rest = start - start.astype(bf16).astype(f32)
        pack_ref[block] = jnp.concatenate([start, rest, place], axis=0).astype(bf16)


def gather_slots(parts, slots_ref):
    count = parts[0].shape[0]
    for i, part in enumerate(parts):
        slots_ref[pl.ds(i * count, count)] = part[...]
    slots_ref[len(parts) * count] = jnp.zeros(slots_ref.shape[1:], bf16)


def position_of(slots_ref, slot, field_rows):
    rows = slots_ref[slot].astype(f32)[field_rows:]
    return rows[:8] + rows[8:] + pltpu.roll(rows[:8], 5, 0)


def turn_positions(slots_ref, first, second, field_rows):
    first = position_of(slots_ref, first, field_rows)
    second = pltpu.roll(position_of(slots_ref, second, field_rows), 3, 0)
    row = lax.broadcasted_iota(jnp.int32, first.shape, 0)
    return jnp.transpose(jnp.where(row < 3, first, second))


def make_tile(home, turned_ref, tiles_ref, pair, half):
    beads = home.shape[1]
    base = half * beads
    for first in range(0, beads, CHUNK):
        turned = turned_ref[pl.ds(first, CHUNK)]
        d = [turned[:, 3 * half + c : 3 * half + c + 1] - home[c : c + 1] for c in range(3)]
        dist_sq = d[0] * d[0] + d[1] * d[1] + d[2] * d[2]
        root = lax.rsqrt(jnp.maximum(dist_sq, 1e-30))
        distance = dist_sq * root
        inv_root = jnp.minimum(root, floor_sq**-0.5)
        inverse_sq = inv_root * inv_root
        far = (0.75 * radius) * inv_root
        far_two = (2.0 * radius * radius) * (far * inverse_sq)
        apart = dist_sq >= 4.0 * radius * radius
        isotropic = jnp.where(apart, far + far_two * (1.0 / 3.0), 1.0 - (9.0 / 32.0 / radius) * distance)
        dyadic = jnp.where(apart, far - far_two, (3.0 / 32.0 / radius) * distance) * inverse_sq
        scaled = [dyadic * d[c] for c in range(3)]
        entries = []
        for c, e in PLACES:
            entry = scaled[c] * d[e]
            entries.append(entry + isotropic if c == e else entry)
        tiles_ref[pair, pl.ds(base + first, CHUNK)] = jnp.concatenate(entries, axis=1).astype(bf16)


def add_product(sum_ref, home, product):
    rows, beads = sum_ref.shape[1:]
    samples = rows // 3
    out = [0.0] * 3
    for k, (c, e) in enumerate(PLACES):
        column = product[:, k * beads : (k + 1) * beads]
        out[c] = out[c] + column[e * samples : (e + 1) * samples]
        if c != e:
            out[e] = out[e] + column[c * samples : (c + 1) * samples]
    sum_ref[home] = sum_ref[home] + jnp.concatenate(out, axis=0)


def field_of(table_ref, slots_ref, first, rows):
    return jnp.concatenate([slots_ref[table_ref[0, first + i]][:rows] for i in range(2)], axis=1)


def product(field, tile):
    return jnp.dot(field, tile, preferred_element_type=f32)


def multiply(table_ref, stage, slots_ref, even_ref, odd_ref, sum_ref):
    blocks, rows = sum_ref.shape[:2]
    count, home_of, first_of = duos_of(table_ref, stage, blocks)

    def both(turn, carry):
        duo = 2 * turn
        odd = jnp.where(duo + 1 < count, turn, 0)
        first = product(field_of(table_ref, slots_ref, first_of(duo), rows), even_ref[turn])
        second = product(field_of(table_ref, slots_ref, first_of(duo + 1), rows), odd_ref[odd])
        add_product(sum_ref, home_of(duo), first)
        add_product(sum_ref, jnp.minimum(home_of(duo + 1), blocks - 1), second)
        return carry

    lax.fori_loop(0, (count + 1) >> 1, both, 0)


def build(table_ref, stage, own_ref, slots_ref, even_ref, odd_ref, sum_ref, turn_even, turn_odd):
    blocks, rows = sum_ref.shape[:2]
    count, home_of, first_of = duos_of(table_ref, stage, blocks)
    odd_ref[0] = jnp.zeros(odd_ref.shape[1:], bf16)

    def prepare(duo, columns_ref):
        first = first_of(duo)
        columns_ref[:, :8] = turn_positions(slots_ref, table_ref[0, first], table_ref[0, first + 1], 2 * rows)

    def consume(duo, tile, index):
        field = field_of(table_ref, slots_ref, first_of(duo), 2 * rows)
        both_parts = product(field, tile[index])
        add_product(sum_ref, jnp.minimum(home_of(duo), blocks - 1), both_parts[:rows] + both_parts[rows:])

    def make(duo, columns_ref, tile, index):
        place = position_of(own_ref, home_of(duo), 2 * rows)
        for i in range(2):
            make_tile(place, columns_ref, tile, index, i)

    def both(turn, spare):
        duo = 2 * turn
        full = duo + 1 < count
        make(duo, turn_even, even_ref, turn)
        prepare(duo + 1, turn_odd)
        consume(jnp.where(turn == 0, count, duo - 1), odd_ref, spare)

        @pl.when(full)
        def _():
            make(duo + 1, turn_odd, odd_ref, turn)
            prepare(duo + 2, turn_even)
            consume(duo, even_ref, turn)

        @pl.when(jnp.logical_not(full))
        def _():
            consume(duo, even_ref, turn)

        return jnp.where(full, turn, spare)

    prepare(0, turn_even)
    spare = lax.fori_loop(0, (count + 1) >> 1, both, 0)
    consume(jnp.where(count % 2 == 0, jnp.maximum(count - 1, 0), count), odd_ref, spare)


def new_field(block, mask_ref, sum_ref, old_ref):
    return sum_ref[block] * mask_ref[block, :1] - old_ref[block]


def stage_kernel(stage, begins, building, moments, *refs):
    refs = list(refs)
    table_ref, own_ref = refs.pop(0), refs.pop(0) if building else None
    tiles = None if building else (refs.pop(0), refs.pop(0))
    before_ref = None if begins else refs.pop(0)
    last = stage == 2
    mask_ref = refs.pop(0) if last else None
    old = [refs.pop(0) for _ in range(3 if moments else 1)] if last else []
    columns = [refs.pop(), refs.pop()] if building else []
    sum_ref = refs.pop() if last else None
    slots_ref = refs.pop()
    outs = [refs.pop() for _ in range(1 if moments or not last else 2)][::-1]
    if building:
        tiles = [refs.pop(), refs.pop()][::-1]
    gather_slots(refs, slots_ref)
    if not last:
        sum_ref = outs[0]
    sum_ref[...] = jnp.zeros_like(sum_ref) if begins else before_ref[...]
    if building:
        build(table_ref, stage, own_ref, slots_ref, *tiles, sum_ref, *columns)
    else:
        multiply(table_ref, stage, slots_ref, *tiles, sum_ref)
    if moments:
        take_moments(mask_ref, sum_ref, *old, outs[0])
    elif last:
        for block in range(sum_ref.shape[0]):
            new = new_field(block, mask_ref, sum_ref, old[0])
            outs[0][block] = new
            outs[1][block] = new.astype(bf16)


MOMENTS = ((0, 0), (0, 1), (1, 1), (1, 2), (2, 2), (2, 3))


def take_moments(mask_ref, sum_ref, x0_ref, x1_ref, x2_ref, moment_ref):
    blocks, rows, beads = x0_ref.shape
    samples = rows // 3
    lanes = moment_ref.shape[2]
    lane = lax.broadcasted_iota(jnp.int32, (samples, lanes), 1)
    row = lax.broadcasted_iota(jnp.int32, (samples, lanes), 0)
    sums = [0.0] * len(MOMENTS)
    for block in range(blocks):
        x = [x0_ref[block], x1_ref[block], x2_ref[block]]
        x.append(new_field(block, mask_ref, sum_ref, x2_ref))
        for k, (i, j) in enumerate(MOMENTS):
            both = x[i] * x[j]
            sums[k] = sums[k] + both[:samples] + both[samples : 2 * samples] + both[2 * samples :]
    grid = jnp.zeros((samples, lanes), f32)
    for k, value in enumerate(sums):
        value = jnp.sum(value, axis=1, keepdims=True)
        grid = jnp.where(lane == row + k * samples, value, grid)
    line = jnp.sum(grid, axis=0, keepdims=True)
    moment_ref[...] = jnp.broadcast_to(line[None], moment_ref.shape)


def inverse_symmetric(m):
    a, b, c, d, e, f = m
    ca, cb, cc = d * f - e * e, c * e - b * f, b * e - c * d
    scale = 1.0 / (a * ca + b * cb + c * cc)
    return (ca * scale, cb * scale, cc * scale, (a * f - c * c) * scale, (b * c - a * e) * scale, (a * d - b * b) * scale)


def final_kernel(moment_ref, x0_ref, x1_ref, x2_ref, out_ref):
    blocks, rows, beads = x0_ref.shape
    samples = rows // 3
    lanes = moment_ref.shape[2]
    lane = lax.broadcasted_iota(jnp.int32, (samples, lanes), 1)
    row = lax.broadcasted_iota(jnp.int32, (samples, lanes), 0)
    line = jnp.broadcast_to(jnp.sum(moment_ref[...], axis=0), (samples, lanes))
    m00, m01, m11, m12, m22, m23 = [
        jnp.broadcast_to(
            jnp.sum(jnp.where(lane == row + k * samples, line, 0.0), axis=1, keepdims=True), (samples, lanes)
        )
        for k in range(len(MOMENTS))
    ]
    norm_sq = m00 + epsilon
    start_norm = jnp.sqrt(norm_sq)
    inv_sq = 1.0 / norm_sq
    alpha1 = (m00 + m01) * inv_sq
    c = 1.0 - alpha1
    res_sq = (m11 + c * (2.0 * m01 + c * m00)) * inv_sq
    beta1 = jnp.sqrt(jnp.maximum(res_sq, 0.0) + epsilon)
    k2 = 1.0 / (start_norm * beta1)
    n11 = m11 + c * (2.0 * m01 + c * m00)
    n12 = m12 + c * (2.0 * m11 + c * m01)
    alpha2 = k2 * k2 * (n11 + n12)
    f1 = 1.0 + c - alpha2
    f0 = c - alpha2 * c - beta1 * beta1
    n22 = m22 + f1 * (2.0 * m12 + f1 * m11) + f0 * (2.0 * (m11 + f1 * m01) + f0 * m00)
    beta2 = jnp.sqrt(jnp.maximum(k2 * k2 * n22, 0.0) + epsilon)
    k3 = k2 / beta2
    n23 = m23 + f1 * (2.0 * m22 + f1 * m12) + f0 * (2.0 * (m12 + f1 * m11) + f0 * m01)
    alpha3 = k3 * k3 * (jnp.maximum(n22, 0.0) + n23)

    scale = (alpha1 + alpha2 + alpha3) / 3.0
    inv_scale = 1.0 / scale
    zero, one = jnp.zeros_like(scale), jnp.ones_like(scale)
    y = (alpha1 * inv_scale, beta1 * inv_scale, zero, alpha2 * inv_scale, beta2 * inv_scale, alpha3 * inv_scale)
    z = (one, zero, zero, one, zero, one)
    for _ in range(ROOT_ITERS):
        inv_z, inv_y = inverse_symmetric(z), inverse_symmetric(y)
        y = tuple(0.5 * (p + q) for p, q in zip(y, inv_z))
        z = tuple(0.5 * (p + q) for p, q in zip(z, inv_y))
    root_scale = jnp.sqrt(scale)
    r1, r2, r3 = root_scale * y[0], root_scale * y[1], root_scale * y[2]
    w2, w3 = start_norm * r2 * k2, start_norm * r3 * k3
    p0 = r1 + w2 * c + w3 * f0
    p1 = w2 + w3 * f1
    for block in range(blocks):
        for c in range(3):
            at = pl.ds(c * samples, samples)
            out = p0 * x0_ref[block, at] + p1 * x1_ref[block, at] + w3 * x2_ref[block, at]
            out_ref[0, 0, block, :, pl.ds(c * beads, beads)] = out


def call(kernel, outs, in_specs, scratch=(), limit=None, cost=None):
    return pl.pallas_call(
        kernel,
        out_shape=outs,
        in_specs=in_specs,
        out_specs=jax.tree.map(lambda _: VMEM, outs),
        scratch_shapes=list(scratch),
        compiler_params=pltpu.CompilerParams(vmem_limit_bytes=limit),
        cost_estimate=cost,
    )


def body(positions, block_fill, noise, pair_list, pair_count):
    blocks, beads = positions.shape[2], positions.shape[4]
    samples = noise.shape[3]
    rows = 3 * samples
    shape = (blocks, rows, beads)
    devices = lax.axis_size(AXES)
    columns = 2 if lax.axis_size("gx") == 2 else 3
    others = 1 if lax.axis_size("gy") == 2 else 2
    sides = 1 if lax.axis_size("gz") == 2 else 2
    at_once = lax.axis_size(("gx", "gy")) <= 8
    middle = others + 1 if at_once else others
    slots = (columns * blocks, middle * columns * blocks, sides * (1 + others) * columns)
    limit = 8 << 20

    x0, mask, packed = call(
        pack_kernel,
        (
            jax.ShapeDtypeStruct(shape, f32),
            jax.ShapeDtypeStruct((blocks, 8, beads), f32),
            jax.ShapeDtypeStruct((blocks, 2 * rows + 16, beads), bf16),
        ),
        [HBM] * 3,
        (
            pltpu.SMEM(block_fill.shape, jnp.int32),
            pltpu.VMEM(noise.shape, f32),
            pltpu.VMEM((1, 1, 3, blocks, beads), f32),
            pltpu.SemaphoreType.DMA((3,)),
        ),
        4 << 20,
    )(*[pltpu.with_memory_space_constraint(a, pltpu.HBM) for a in (block_fill, noise, jnp.swapaxes(positions, 2, 3))])
    table = pair_table(pair_list, pair_count, blocks, slots, columns, at_once)
    field, sent = jax.ShapeDtypeStruct(shape, f32), jax.ShapeDtypeStruct(shape, bf16)
    capacity = (pair_list.shape[4] + blocks) // 4 + 1
    tile = jax.ShapeDtypeStruct((capacity, 2 * beads, len(PLACES) * beads), bf16)
    total = pltpu.VMEM(shape, f32)
    moment = jax.ShapeDtypeStruct((devices, 1, 128), f32)
    cost = pl.CostEstimate(flops=10**8, bytes_accessed=10**7, transcendentals=0)

    def apply(vector, tiles, olds):
        building, moments = not tiles, len(olds) == 3

        def stage(table, index, given, result):
            last = index == 2
            outs = (moment,) if last and moments else (field, sent) if last else (field,)
            scratch = [pltpu.VMEM((slots[index] + 1,) + given[0].shape[1:], bf16)]
            scratch += [total] * last + [pltpu.VMEM((beads, 128), f32)] * (2 * building)
            args = [packed] if building else list(tiles[index])
            args += ([] if result is None else [result]) + ([mask] + olds if last else []) + given
            result = call(
                functools.partial(stage_kernel, index, result is None, building, last and moments),
                (tile, tile) * building + outs,
                [SMEM] + [VMEM] * len(args),
                scratch,
                limit,
                None if last else cost,
            )(table, *args)
            if building:
                tiles[index] = result[:2]
                result = result[2:]
            return result if last and not moments else result[0]

        return spread(vector, table, stage, at_once)

    tiles = {}
    x1, send = apply(packed, tiles, [x0])
    x2, send = apply(send, tiles, [x1])
    moments = apply(send, tiles, [x0, x1, x2])
    moments = lax.all_to_all(moments, AXES, 0, 0)
    return call(final_kernel, jax.ShapeDtypeStruct(noise.shape, f32), [VMEM] * 4, (), 4 << 20)(moments, x0, x1, x2)


def solution(mesh):
    block = P("gx", "gy", "gz", None, None)
    cell = P("gx", "gy", "gz")
    return jax.shard_map(
        body, mesh=mesh, in_specs=(block, cell, block, block, cell), out_specs=block, check_vma=False
    )
```

```python
import functools

import jax
import jax.numpy as jnp
from jax import lax
from jax.experimental import pallas as pl
from jax.experimental.pallas import tpu as pltpu
from jax.sharding import PartitionSpec as P

ITERS = 3
ROOT_ITERS = 12
CHUNK = 16

radius = 0.08
floor_sq = 0.0001
epsilon = 1e-06

AXES = ("gx", "gy", "gz")
VMEM = pl.BlockSpec(memory_space=pltpu.VMEM)
HBM = pl.BlockSpec(memory_space=pltpu.HBM)
SMEM = pl.BlockSpec(memory_space=pltpu.SMEM)
f32 = jnp.float32
bf16 = jnp.bfloat16
PLACES = ((0, 0), (0, 1), (0, 2), (1, 1), (1, 2), (2, 2))


def matching(count, parity):
    pairs = []
    for i in range(parity, count - 1, 2):
        pairs += [(i, i + 1), (i + 1, i)]
    return pairs


def swaps(axis, first, second):
    count = lax.axis_size(axis)
    got = [lax.ppermute(first, axis, matching(count, 0))]
    if count > 2:
        got.append(lax.ppermute(second, axis, matching(count, 1)))
    return got


def plane_exchange(field, wide):
    plane = ("gx", "gy")
    size_x, size_y = [lax.axis_size(axis) for axis in plane]
    if wide is None:
        wide = jnp.broadcast_to(field[None], (size_x * size_y,) + field.shape)
    got = lax.all_to_all(wide, plane, 0, 0)
    x, y = [lax.axis_index(axis) for axis in plane]

    def partners(index, count):
        even, odd = index + 1 - 2 * (index % 2), index - 1 + 2 * (index % 2)
        return [index, jnp.minimum(even, count - 1)] + [jnp.clip(odd, 0, count - 1)] * (count > 2)

    rows = [
        jnp.stack([lax.dynamic_index_in_dim(got, i * size_y + j, 0, False) for i in partners(x, size_x)])
        for j in partners(y, size_y)
    ]
    return rows[0], rows[1:]


def spread(field, table, stage, at_once, wide):
    shape = (-1,) + field.shape[1:]
    if at_once:
        columns, others = plane_exchange(field, wide)
    else:
        columns = jnp.stack([field] + swaps("gx", field, field))
        columns, table = lax.optimization_barrier((columns, table))
        others = swaps("gy", columns, columns)
    rows = [part.reshape(shape) for part in [columns] + others]
    result = None if at_once else stage(table, 0, rows[:1], None)
    odd = lax.axis_index("gz") % 2 == 1
    low = jnp.concatenate([part[:, 0] for part in [columns] + others])
    high = jnp.concatenate([part[:, field.shape[0] - 1] for part in [columns] + others])
    low, high = jnp.where(odd, low, high), jnp.where(odd, high, low)
    if not at_once:
        low, high, result = lax.optimization_barrier((low, high, result))
    far = swaps("gz", low, high)
    result = stage(table, 1, rows if at_once else rows[1:], result)
    return stage(table, 2, far, result)


def table_kernel(sizes, slots, width, at_once, blocks, count_ref, list_hbm, table_ref, list_ref, sem):
    copy = pltpu.make_async_copy(list_hbm, list_ref, sem)
    copy.start()
    sets = len(slots) * blocks
    segment = table_ref.shape[1] // sets
    for i in range(sets):
        table_ref[1, i] = 0
    odd = [lax.rem(lax.axis_index(axis), 2) == 1 for axis in AXES]

    def partner(axis, step):
        if sizes[axis] == 2:
            return jnp.where(step == 0, 0, 1)
        return jnp.where(step == 0, 0, jnp.where((step < 0) == odd[axis], 1, 2))

    def enter(t, carry):
        home, code = list_ref[0, 0, 0, 0, t], list_ref[0, 0, 1, 0, t]
        plane, third = (code * 57) >> 9, (code * 43) >> 7
        x, y = partner(0, plane - 1), partner(1, third - 3 * plane - 1)
        z = home + code - 3 * third - 1
        far = (z < 0) | (z >= blocks)
        side = partner(2, jnp.where(z < 0, -1, 1)) - 1
        row = y if at_once else jnp.maximum(y - 1, 0)
        slot = (row * width + x) * blocks + z
        slot = jnp.where(far, side * (slots[2] // (1 if sizes[2] == 2 else 2)) + y * width + x, slot)
        at = jnp.where(far, 2, 1 if at_once else jnp.minimum(y, 1)) * blocks + home
        place = table_ref[1, at]
        table_ref[1, at] = place + 1
        table_ref[0, at * segment + place] = slot
        return carry

    copy.wait()
    lax.fori_loop(0, count_ref[0, 0, 0], enter, 0)
    for stage, empty in enumerate(slots):
        for block in range(blocks):
            at = stage * blocks + block
            end = at * segment + table_ref[1, at]
            for i in range(3):
                table_ref[0, end + i] = empty


def pair_table(pair_list, pair_count, blocks, slots, width, at_once):
    segment = -(-(pair_list.shape[4] + 3) // 2) * 2
    sizes = [lax.axis_size(axis) for axis in AXES]
    pair_list = pltpu.with_memory_space_constraint(jnp.swapaxes(pair_list, 2, 3), pltpu.HBM)
    return pl.pallas_call(
        functools.partial(table_kernel, sizes, slots, width, at_once, blocks),
        out_shape=jax.ShapeDtypeStruct((2, len(slots) * blocks * segment), jnp.int32),
        in_specs=[SMEM, HBM],
        out_specs=SMEM,
        scratch_shapes=[pltpu.SMEM(pair_list.shape, jnp.int32), pltpu.SemaphoreType.DMA],
        compiler_params=pltpu.CompilerParams(vmem_limit_bytes=1 << 20),
        cost_estimate=pl.CostEstimate(flops=10**6, bytes_accessed=10**6, transcendentals=0),
    )(pair_count, pair_list)


def duos_of(table_ref, stage, blocks):
    segment = table_ref.shape[1] // (3 * blocks)
    counts = [(table_ref[1, stage * blocks + block] + 1) >> 1 for block in range(blocks)]
    ends = [sum(counts[: block + 1]) for block in range(blocks)]

    def home_of(duo):
        return sum([jnp.where(duo >= end, 1, 0) for end in ends[:-1]], 0)

    def first_of(duo):
        skip = [jnp.where(duo >= ends[i], segment - 2 * counts[i], 0) for i in range(blocks - 1)]
        return stage * blocks * segment + 2 * duo + sum(skip)

    return ends[-1], home_of, first_of


def pack_kernel(fill_hbm, noise_hbm, pos_hbm, start_ref, mask_ref, pack_ref, wide_ref, fill_ref, noise_ref, pos_ref, sems):
    pairs = ((fill_hbm, fill_ref), (noise_hbm, noise_ref), (pos_hbm, pos_ref))
    copies = [pltpu.make_async_copy(a, b, sems.at[i]) for i, (a, b) in enumerate(pairs)]
    for copy in copies:
        copy.start()
    for copy in copies:
        copy.wait()
    blocks, samples, width = noise_ref.shape[2:]
    beads = width // 3
    row = lax.broadcasted_iota(jnp.int32, (16, beads), 0)
    for block in range(blocks):
        mask = (lax.broadcasted_iota(jnp.int32, (8, beads), 1) < fill_ref[0, 0, block]).astype(f32)
        mask_ref[block] = mask
        noise = [noise_ref[0, 0, block, :, pl.ds(c * beads, beads)] for c in range(3)]
        start = jnp.concatenate([part * mask[:1] for part in noise], axis=0)
        start_ref[block] = start
        place = jnp.zeros((16, beads), f32)
        for c in range(3):
            pos = pos_ref[0, 0, c, pl.ds(block, 1)]
            high = pos.astype(bf16).astype(f32)
            rest = pos - high
            mid = rest.astype(bf16).astype(f32)
            for i, piece in ((0, high), (8, mid), (3, rest - mid)):
                place = jnp.where(row == i + c, piece, place)
        packed = jnp.concatenate([start, place], axis=0).astype(bf16)
        pack_ref[block] = packed
        for copy in range(wide_ref.shape[0]):
            wide_ref[copy, block] = packed


def gather_slots(parts, slots_ref):
    count = parts[0].shape[0]
    for i, part in enumerate(parts):
        slots_ref[pl.ds(i * count, count)] = part[...]
    slots_ref[len(parts) * count] = jnp.zeros(slots_ref.shape[1:], bf16)


def position_of(slots_ref, slot, field_rows):
    rows = slots_ref[slot].astype(f32)[field_rows:]
    return rows[:8] + rows[8:] + pltpu.roll(rows[:8], 5, 0)


def turn_positions(slots_ref, first, second, field_rows):
    first = position_of(slots_ref, first, field_rows)
    second = pltpu.roll(position_of(slots_ref, second, field_rows), 3, 0)
    row = lax.broadcasted_iota(jnp.int32, first.shape, 0)
    return jnp.transpose(jnp.where(row < 3, first, second))


def make_tile(home, turned_ref, tiles_ref, pair, half):
    beads = home.shape[1]
    base = half * beads
    for first in range(0, beads, CHUNK):
        turned = turned_ref[pl.ds(first, CHUNK)]
        d = [turned[:, 3 * half + c : 3 * half + c + 1] - home[c : c + 1] for c in range(3)]
        dist_sq = d[0] * d[0] + d[1] * d[1] + d[2] * d[2]
        root = lax.rsqrt(jnp.maximum(dist_sq, 1e-30))
        distance = dist_sq * root
        inv_root = jnp.minimum(root, floor_sq**-0.5)
        inverse_sq = inv_root * inv_root
        far = (0.75 * radius) * inv_root
        far_two = (2.0 * radius * radius) * (far * inverse_sq)
        apart = dist_sq >= 4.0 * radius * radius
        isotropic = jnp.where(apart, far + far_two * (1.0 / 3.0), 1.0 - (9.0 / 32.0 / radius) * distance)
        dyadic = jnp.where(apart, far - far_two, (3.0 / 32.0 / radius) * distance) * inverse_sq
        scaled = [dyadic * d[c] for c in range(3)]
        entries = []
        for c, e in PLACES:
            entry = scaled[c] * d[e]
            entries.append(entry + isotropic if c == e else entry)
        tiles_ref[pair, pl.ds(base + first, CHUNK)] = jnp.concatenate(entries, axis=1).astype(bf16)


def add_product(sum_ref, home, product):
    rows, beads = sum_ref.shape[1:]
    samples = rows // 3
    out = [0.0] * 3
    for k, (c, e) in enumerate(PLACES):
        column = product[:, k * beads : (k + 1) * beads]
        out[c] = out[c] + column[e * samples : (e + 1) * samples]
        if c != e:
            out[e] = out[e] + column[c * samples : (c + 1) * samples]
    sum_ref[home] = sum_ref[home] + jnp.concatenate(out, axis=0)


def field_of(table_ref, slots_ref, first, rows):
    return jnp.concatenate([slots_ref[table_ref[0, first + i]][:rows] for i in range(2)], axis=1)


def product(field, tile):
    return jnp.dot(field, tile, preferred_element_type=f32)


def multiply(table_ref, stage, slots_ref, even_ref, odd_ref, sum_ref):
    blocks, rows = sum_ref.shape[:2]
    count, home_of, first_of = duos_of(table_ref, stage, blocks)

    def both(turn, carry):
        duo = 2 * turn
        odd = jnp.where(duo + 1 < count, turn, 0)
        first = product(field_of(table_ref, slots_ref, first_of(duo), rows), even_ref[turn])
        second = product(field_of(table_ref, slots_ref, first_of(duo + 1), rows), odd_ref[odd])
        add_product(sum_ref, home_of(duo), first)
        add_product(sum_ref, jnp.minimum(home_of(duo + 1), blocks - 1), second)
        return carry

    lax.fori_loop(0, (count + 1) >> 1, both, 0)


def build(table_ref, stage, own_ref, slots_ref, even_ref, odd_ref, sum_ref, turn_even, turn_odd):
    blocks, rows = sum_ref.shape[:2]
    count, home_of, first_of = duos_of(table_ref, stage, blocks)
    odd_ref[0] = jnp.zeros(odd_ref.shape[1:], bf16)

    def prepare(duo, columns_ref):
        first = first_of(duo)
        columns_ref[:, :8] = turn_positions(slots_ref, table_ref[0, first], table_ref[0, first + 1], rows)

    def consume(duo, tile, index):
        field = field_of(table_ref, slots_ref, first_of(duo), rows)
        add_product(sum_ref, jnp.minimum(home_of(duo), blocks - 1), product(field, tile[index]))

    def make(duo, columns_ref, tile, index):
        place = position_of(own_ref, home_of(duo), rows)
        for i in range(2):
            make_tile(place, columns_ref, tile, index, i)

    def both(turn, spare):
        duo = 2 * turn
        full = duo + 1 < count
        make(duo, turn_even, even_ref, turn)
        prepare(duo + 1, turn_odd)
        consume(jnp.where(turn == 0, count, duo - 1), odd_ref, spare)

        @pl.when(full)
        def _():
            make(duo + 1, turn_odd, odd_ref, turn)
            prepare(duo + 2, turn_even)
            consume(duo, even_ref, turn)

        @pl.when(jnp.logical_not(full))
        def _():
            consume(duo, even_ref, turn)

        return jnp.where(full, turn, spare)

    prepare(0, turn_even)
    spare = lax.fori_loop(0, (count + 1) >> 1, both, 0)
    consume(jnp.where(count % 2 == 0, jnp.maximum(count - 1, 0), count), odd_ref, spare)


def new_field(block, mask_ref, sum_ref, old_ref):
    return sum_ref[block] * mask_ref[block, :1] - old_ref[block]


def stage_kernel(stage, begins, building, moments, *refs):
    refs = list(refs)
    table_ref, own_ref = refs.pop(0), refs.pop(0) if building else None
    tiles = None if building else (refs.pop(0), refs.pop(0))
    before_ref = None if begins else refs.pop(0)
    last = stage == 2
    mask_ref = refs.pop(0) if last else None
    old = [refs.pop(0) for _ in range(3 if moments else 1)] if last else []
    columns = [refs.pop(), refs.pop()] if building else []
    sum_ref = refs.pop() if last else None
    slots_ref = refs.pop()
    outs = [refs.pop() for _ in range(1 if moments or not last else 2)][::-1]
    if building:
        tiles = [refs.pop(), refs.pop()][::-1]
    gather_slots(refs, slots_ref)
    if not last:
        sum_ref = outs[0]
    sum_ref[...] = jnp.zeros_like(sum_ref) if begins else before_ref[...]
    if building:
        build(table_ref, stage, own_ref, slots_ref, *tiles, sum_ref, *columns)
    else:
        multiply(table_ref, stage, slots_ref, *tiles, sum_ref)
    if moments:
        take_moments(mask_ref, sum_ref, *old, outs[0])
    elif last:
        for block in range(sum_ref.shape[0]):
            new = new_field(block, mask_ref, sum_ref, old[0])
            outs[0][block] = new
            outs[1][block] = new.astype(bf16)


MOMENTS = ((0, 0), (0, 1), (1, 1), (1, 2), (2, 2), (2, 3))


def take_moments(mask_ref, sum_ref, x0_ref, x1_ref, x2_ref, moment_ref):
    blocks, rows, beads = x0_ref.shape
    samples = rows // 3
    lanes = moment_ref.shape[2]
    lane = lax.broadcasted_iota(jnp.int32, (samples, lanes), 1)
    row = lax.broadcasted_iota(jnp.int32, (samples, lanes), 0)
    sums = [0.0] * len(MOMENTS)
    for block in range(blocks):
        x = [x0_ref[block], x1_ref[block], x2_ref[block]]
        x.append(new_field(block, mask_ref, sum_ref, x2_ref))
        for k, (i, j) in enumerate(MOMENTS):
            both = x[i] * x[j]
            sums[k] = sums[k] + both[:samples] + both[samples : 2 * samples] + both[2 * samples :]
    grid = jnp.zeros((samples, lanes), f32)
    for k, value in enumerate(sums):
        value = jnp.sum(value, axis=1, keepdims=True)
        grid = jnp.where(lane == row + k * samples, value, grid)
    line = jnp.sum(grid, axis=0, keepdims=True)
    moment_ref[...] = jnp.broadcast_to(line[None], moment_ref.shape)


def inverse_symmetric(m):
    a, b, c, d, e, f = m
    ca, cb, cc = d * f - e * e, c * e - b * f, b * e - c * d
    scale = 1.0 / (a * ca + b * cb + c * cc)
    return (ca * scale, cb * scale, cc * scale, (a * f - c * c) * scale, (b * c - a * e) * scale, (a * d - b * b) * scale)


def final_kernel(moment_ref, x0_ref, x1_ref, x2_ref, out_ref):
    blocks, rows, beads = x0_ref.shape
    samples = rows // 3
    lanes = moment_ref.shape[2]
    lane = lax.broadcasted_iota(jnp.int32, (samples, lanes), 1)
    row = lax.broadcasted_iota(jnp.int32, (samples, lanes), 0)
    line = jnp.broadcast_to(jnp.sum(moment_ref[...], axis=0), (samples, lanes))
    m00, m01, m11, m12, m22, m23 = [
        jnp.broadcast_to(
            jnp.sum(jnp.where(lane == row + k * samples, line, 0.0), axis=1, keepdims=True), (samples, lanes)
        )
        for k in range(len(MOMENTS))
    ]
    norm_sq = m00 + epsilon
    start_norm = jnp.sqrt(norm_sq)
    inv_sq = 1.0 / norm_sq
    alpha1 = (m00 + m01) * inv_sq
    c = 1.0 - alpha1
    res_sq = (m11 + c * (2.0 * m01 + c * m00)) * inv_sq
    beta1 = jnp.sqrt(jnp.maximum(res_sq, 0.0) + epsilon)
    k2 = 1.0 / (start_norm * beta1)
    n11 = m11 + c * (2.0 * m01 + c * m00)
    n12 = m12 + c * (2.0 * m11 + c * m01)
    alpha2 = k2 * k2 * (n11 + n12)
    f1 = 1.0 + c - alpha2
    f0 = c - alpha2 * c - beta1 * beta1
    n22 = m22 + f1 * (2.0 * m12 + f1 * m11) + f0 * (2.0 * (m11 + f1 * m01) + f0 * m00)
    beta2 = jnp.sqrt(jnp.maximum(k2 * k2 * n22, 0.0) + epsilon)
    k3 = k2 / beta2
    n23 = m23 + f1 * (2.0 * m22 + f1 * m12) + f0 * (2.0 * (m12 + f1 * m11) + f0 * m01)
    alpha3 = k3 * k3 * (jnp.maximum(n22, 0.0) + n23)

    scale = (alpha1 + alpha2 + alpha3) / 3.0
    inv_scale = 1.0 / scale
    zero, one = jnp.zeros_like(scale), jnp.ones_like(scale)
    y = (alpha1 * inv_scale, beta1 * inv_scale, zero, alpha2 * inv_scale, beta2 * inv_scale, alpha3 * inv_scale)
    z = (one, zero, zero, one, zero, one)
    for _ in range(ROOT_ITERS):
        inv_z, inv_y = inverse_symmetric(z), inverse_symmetric(y)
        y = tuple(0.5 * (p + q) for p, q in zip(y, inv_z))
        z = tuple(0.5 * (p + q) for p, q in zip(z, inv_y))
    root_scale = jnp.sqrt(scale)
    r1, r2, r3 = root_scale * y[0], root_scale * y[1], root_scale * y[2]
    w2, w3 = start_norm * r2 * k2, start_norm * r3 * k3
    p0 = r1 + w2 * c + w3 * f0
    p1 = w2 + w3 * f1
    for block in range(blocks):
        for c in range(3):
            at = pl.ds(c * samples, samples)
            out = p0 * x0_ref[block, at] + p1 * x1_ref[block, at] + w3 * x2_ref[block, at]
            out_ref[0, 0, block, :, pl.ds(c * beads, beads)] = out


def call(kernel, outs, in_specs, scratch=(), limit=None, cost=None):
    return pl.pallas_call(
        kernel,
        out_shape=outs,
        in_specs=in_specs,
        out_specs=jax.tree.map(lambda _: VMEM, outs),
        scratch_shapes=list(scratch),
        compiler_params=pltpu.CompilerParams(vmem_limit_bytes=limit),
        cost_estimate=cost,
    )


def body(positions, block_fill, noise, pair_list, pair_count):
    blocks, beads = positions.shape[2], positions.shape[4]
    samples = noise.shape[3]
    rows = 3 * samples
    shape = (blocks, rows, beads)
    devices = lax.axis_size(AXES)
    columns = 2 if lax.axis_size("gx") == 2 else 3
    others = 1 if lax.axis_size("gy") == 2 else 2
    sides = 1 if lax.axis_size("gz") == 2 else 2
    at_once = lax.axis_size(("gx", "gy")) <= 8
    middle = others + 1 if at_once else others
    slots = (columns * blocks, middle * columns * blocks, sides * (1 + others) * columns)
    limit = 8 << 20

    wide = lax.axis_size(("gx", "gy")) if at_once else 1
    x0, mask, packed, packed_wide = call(
        pack_kernel,
        (
            jax.ShapeDtypeStruct(shape, f32),
            jax.ShapeDtypeStruct((blocks, 8, beads), f32),
            jax.ShapeDtypeStruct((blocks, rows + 16, beads), bf16),
            jax.ShapeDtypeStruct((wide, blocks, rows + 16, beads), bf16),
        ),
        [HBM] * 3,
        (
            pltpu.SMEM(block_fill.shape, jnp.int32),
            pltpu.VMEM(noise.shape, f32),
            pltpu.VMEM((1, 1, 3, blocks, beads), f32),
            pltpu.SemaphoreType.DMA((3,)),
        ),
        4 << 20,
    )(*[pltpu.with_memory_space_constraint(a, pltpu.HBM) for a in (block_fill, noise, jnp.swapaxes(positions, 2, 3))])
    table = pair_table(pair_list, pair_count, blocks, slots, columns, at_once)
    field, sent = jax.ShapeDtypeStruct(shape, f32), jax.ShapeDtypeStruct(shape, bf16)
    capacity = (pair_list.shape[4] + blocks) // 4 + 1
    tile = jax.ShapeDtypeStruct((capacity, 2 * beads, len(PLACES) * beads), bf16)
    total = pltpu.VMEM(shape, f32)
    moment = jax.ShapeDtypeStruct((devices, 1, 128), f32)
    cost = pl.CostEstimate(flops=10**8, bytes_accessed=10**7, transcendentals=0)

    def apply(vector, tiles, olds):
        building, moments = not tiles, len(olds) == 3

        def stage(table, index, given, result):
            last = index == 2
            outs = (moment,) if last and moments else (field, sent) if last else (field,)
            scratch = [pltpu.VMEM((slots[index] + 1,) + given[0].shape[1:], bf16)]
            scratch += [total] * last + [pltpu.VMEM((beads, 128), f32)] * (2 * building)
            args = [packed] if building else list(tiles[index])
            args += ([] if result is None else [result]) + ([mask] + olds if last else []) + given
            result = call(
                functools.partial(stage_kernel, index, result is None, building, last and moments),
                (tile, tile) * building + outs,
                [SMEM] + [VMEM] * len(args),
                scratch,
                limit,
                None if last else cost,
            )(table, *args)
            if building:
                tiles[index] = result[:2]
                result = result[2:]
            return result if last and not moments else result[0]

        return spread(vector, table, stage, at_once, packed_wide if building else None)

    tiles = {}
    x1, send = apply(packed, tiles, [x0])
    x2, send = apply(send, tiles, [x1])
    moments = apply(send, tiles, [x0, x1, x2])
    moments = lax.all_to_all(moments, AXES, 0, 0)
    return call(final_kernel, jax.ShapeDtypeStruct(noise.shape, f32), [VMEM] * 4, (), 4 << 20)(moments, x0, x1, x2)


def solution(mesh):
    block = P("gx", "gy", "gz", None, None)
    cell = P("gx", "gy", "gz")
    return jax.shard_map(
        body, mesh=mesh, in_specs=(block, cell, block, block, cell), out_specs=block, check_vma=False
    )
```
